32 devices in a mesh: group: 2 (over x), expert: 8 (over z, y), cuts: 2 (over core).
Axes of the slice: x: 2, y: 2, z: 4, core: 2. Of those that a mesh axis runs over, the one named last changes fastest.
Arguments:
- x_in: bfloat16 [512, 4096], P(('group', 'expert'), 'cuts'), parts along dimension 0, may hold values from -6 to 6
- routes: int32 [512, 2], P(('group', 'expert')), parts along dimension 0, may hold values from 0 to 15, as said below
- conv_state: float32 [64, 3, 4096], P('group', None, ('expert', 'cuts')), parts along dimension 0, may hold values from -6 to 6
- ssm_state: float32 [64, 16, 4096], P('group', None, ('expert', 'cuts')), parts along dimension 0, may hold values from -6 to 6
- mamba_gain: float32 [4096], replicated, may hold values from 0.1 to 1.9
- in_x: bfloat16 [4096, 4096], P(None, ('expert', 'cuts')), may hold values from -0.09375 to 0.09375
- in_z: bfloat16 [4096, 4096], P(None, ('expert', 'cuts')), may hold values from -0.09375 to 0.09375
- conv_w: float32 [4, 4096], P(None, ('expert', 'cuts')), may hold values from -3 to 3
- conv_b: float32 [4096], P(('expert', 'cuts')), may hold values from -3 to 3
- xproj_dt: bfloat16 [4096, 512], P(('expert', 'cuts')), may hold values from -0.09375 to 0.09375
- xproj_bc: bfloat16 [4096, 32], P(('expert', 'cuts')), may hold values from -0.09375 to 0.09375
- dt_proj: bfloat16 [512, 4096], P(None, ('expert', 'cuts')), may hold values from -0.25 to 0.25
- dt_bias: float32 [4096], P(('expert', 'cuts')), may hold values from -4 to 0
- a_rate: float32 [16, 4096], P(None, ('expert', 'cuts')), may hold values from 0.5 to 16
- d_skip: float32 [4096], P(('expert', 'cuts')), may hold values from 0.5 to 1.5
- out_proj: bfloat16 [4096, 4096], P(('expert', 'cuts')), may hold values from -0.09375 to 0.09375
- moe_gain: float32 [4096], replicated, may hold values from 0.1 to 1.9
- router: bfloat16 [4096, 16], replicated, may hold values from -0.09375 to 0.09375
- w_gate: bfloat16 [4096, 12288], P(None, ('expert', 'cuts')), may hold values from -0.09375 to 0.09375
- w_up: bfloat16 [4096, 12288], P(None, ('expert', 'cuts')), may hold values from -0.09375 to 0.09375
- w_down: bfloat16 [12288, 4096], P(('expert', 'cuts')), may hold values from -0.078125 to 0.078125
Outputs:
- stream_out: bfloat16 [512, 4096], P(('group', 'expert'), 'cuts'), parts along dimension 0
- new_state: float32 [64, 16, 4096], P('group', None, ('expert', 'cuts')), parts along dimension 0
The draws below stay inside these ranges and needn't reach their ends.
There are 2 independent parts, one for each index of `group`. The reference program is written for one: setup_inputs(seed, part) draws one part's arguments, and reference() takes and returns one part's arrays. A program takes and returns all parts, laid end to end along the dimension named above; an argument that names none is the same for every part. Nothing has to cross between parts.
Inputs may be any that keep to these rules, and one draw needn't show every extreme that they name: `routes`: each token names 2 different experts. Among the 32 tokens of one index of expert (aligned blocks of rows), at most 16 name any one expert below 2, and in every block one of them is named by exactly 16; no token names two experts below 2.
All inputs are finite; a program needn't handle non-finite values.
Results may differ from the reference program's by a relative error of at most 0.0095.
Values may be sent and summed in bfloat16 or wider, within the bound.
No kernel may reach another device: no remote copies, remote signals or barrier semaphores. Data moves between devices by JAX's collectives and lax.ppermute only.
A program may use at most 128 MiB of HBM per device.

```python
import math
import jax
import jax.numpy as jnp
from jax import lax

D = 4096
R = 512
N = 16
TOPK = 2
EXPERTS_ALL = 16
EXPERTS = 2
DRAFT = 8
TOK_DEV = 32
CAP = 16
REQS = 32
TOKENS = 256
CH = 4096
HID = 6144
N_EXPERT = 8


def draw_routes(key, part):
    blocks = TOKENS // TOK_DEV
    keys = jax.random.split(jax.random.fold_in(key, 7), 6)
    hot = jax.random.randint(keys[0], (blocks, 1), 0, EXPERTS)
    others = jax.random.randint(keys[1], (blocks, EXPERTS), 1, CAP + 1)
    labels = jnp.arange(EXPERTS, dtype=jnp.int32)
    counts = jnp.where(labels[None, :] == hot, CAP, others).astype(jnp.int32)
    bounds = jnp.cumsum(counts, axis=1)
    perms = jax.vmap(lambda k: jax.random.permutation(k, TOK_DEV))(jax.random.split(keys[2], blocks))
    rank_of = jnp.argsort(perms, axis=1).astype(jnp.int32)
    window = jnp.sum((rank_of[:, :, None] >= bounds[:, None, :]).astype(jnp.int32), axis=-1)
    assigned = window < EXPERTS
    outer = EXPERTS_ALL - EXPERTS
    first_out = jax.random.randint(keys[3], (blocks, TOK_DEV), 0, outer)
    offset = jax.random.randint(keys[4], (blocks, TOK_DEV), 1, outer)
    second_out = (first_out + offset) % outer
    first_out = first_out + EXPERTS
    second_out = second_out + EXPERTS
    first = jnp.where(assigned, window, first_out)
    second = jnp.where(assigned, first_out, second_out)
    flip = jax.random.randint(keys[5], (blocks, TOK_DEV), 0, 2)
    route0 = jnp.where(flip == 1, second, first)
    route1 = jnp.where(flip == 1, first, second)
    return jnp.stack([route0, route1], axis=-1).reshape(TOKENS, TOPK).astype(jnp.int32)


def block_scale(own_key, dims, pieces, low, high):
    level, own = 1.0, jax.random.fold_in(own_key, 6)
    for position, parts in pieces:
        steps = jnp.exp(jax.random.uniform(jax.random.fold_in(own, position), (parts,), jnp.float32, low / len(pieces), high / len(pieces)))
        level = level * jnp.repeat(steps, dims[position] // parts).reshape([-1 if axis == position else 1 for axis in range(len(dims))])
    return level


def scatter_about(key, dims, width, bound, pieces=(), kind=jnp.bfloat16):
    level = block_scale(key, dims, pieces, -0.22, 0.18) if pieces else 1.0
    drawn = jax.random.normal(key, dims, jnp.float32) * width * level
    return jnp.minimum(jnp.maximum(drawn, -bound), bound).astype(kind)


def setup_inputs(seed: int = 0, part: int = 0) -> dict:
    splits = jax.random.split(jax.random.key(seed), 22)
    part_keys = jax.random.split(jax.random.fold_in(splits[21], part), 22)
    return {
        "x_in": scatter_about(part_keys[0], (TOKENS, D), 1.0, 6.0, ((0, 8), (1, 2))),
        "routes": draw_routes(jax.random.fold_in(jax.random.fold_in(splits[21], part), 71), part),
        "conv_state": scatter_about(part_keys[2], (REQS, 3, CH), 1.0, 6.0, ((2, 16),), jnp.float32),
        "ssm_state": scatter_about(part_keys[3], (REQS, N, CH), 1.0, 6.0, ((2, 16),), jnp.float32),
        "mamba_gain": jnp.clip(1.0 + 0.18 * jax.random.normal(splits[4], (D,), jnp.float32), 0.1, 1.9),
        "in_x": scatter_about(splits[5], (D, CH), D ** -0.5, 0.09375, ((1, 16),)),
        "in_z": scatter_about(splits[6], (D, CH), D ** -0.5, 0.09375, ((1, 16),)),
        "conv_w": scatter_about(splits[7], (4, CH), 4 ** -0.5, 3.0, ((1, 16),), jnp.float32),
        "conv_b": scatter_about(splits[8], (CH,), 0.5, 3.0, ((0, 16),), jnp.float32),
        "xproj_dt": scatter_about(splits[9], (CH, R), CH ** -0.5, 0.09375, ((0, 16),)),
        "xproj_bc": scatter_about(splits[10], (CH, 2 * N), CH ** -0.5, 0.09375, ((0, 16),)),
        "dt_proj": scatter_about(splits[11], (R, CH), R ** -0.5, 0.25, ((1, 16),)),
        "dt_bias": jnp.clip(-4.0 + 4.0 * jax.random.uniform(splits[12], (CH,), jnp.float32) ** block_scale(splits[12], (CH,), ((0, 16),), -0.2, 0.2), -4.0, 0.0),
        "a_rate": jnp.clip(jnp.exp(math.log(16.0) - 3.465736 * jax.random.uniform(splits[13], (N, CH), jnp.float32) ** block_scale(splits[13], (N, CH), ((1, 16),), -0.2, 0.2)), 0.5, 16.0),
        "d_skip": jnp.clip(0.5 + 1.0 * jax.random.uniform(splits[14], (CH,), jnp.float32) ** block_scale(splits[14], (CH,), ((0, 16),), -0.2, 0.2), 0.5, 1.5),
        "out_proj": scatter_about(splits[15], (CH, D), CH ** -0.5, 0.09375, ((0, 16),)),
        "moe_gain": jnp.clip(1.0 + 0.18 * jax.random.normal(splits[16], (D,), jnp.float32), 0.1, 1.9),
        "router": scatter_about(splits[17], (D, EXPERTS_ALL), D ** -0.5, 0.09375),
        "w_gate": scatter_about(splits[18], (D, EXPERTS * HID), D ** -0.5, 0.09375, ((1, 16),)),
        "w_up": scatter_about(splits[19], (D, EXPERTS * HID), D ** -0.5, 0.09375, ((1, 16),)),
        "w_down": scatter_about(splits[20], (EXPERTS * HID, D), HID ** -0.5, 0.078125, ((0, 16),)),
    }


def rms_norm(values, gain):
    values = values.astype(jnp.float32)
    scale = lax.rsqrt(lax.optimization_barrier(jnp.mean(values * values, axis=-1, keepdims=True)) + 1e-05)
    return (values * scale * gain).astype(jnp.bfloat16)

def ssm_steps(inputs, steps, b_maps, c_maps, state, a_rate, d_skip):
    outputs = []
    for place in range(inputs.shape[1]):
        decay = jnp.exp(-steps[:, place, None, :] * a_rate[None])
        state = decay * state + (steps[:, place] * inputs[:, place])[:, None, :] * b_maps[:, place, :, None]
        outputs.append(lax.optimization_barrier(jnp.sum(c_maps[:, place, :, None] * state, axis=1)) + d_skip * inputs[:, place])
    return (jnp.stack(outputs, axis=1), state)

def place_rows(dest, rows):
    table = jnp.zeros((EXPERTS * CAP + 1, rows.shape[1]), jnp.bfloat16).at[dest].set(rows)
    return table[:EXPERTS * CAP]

def take_rows(table, dest):
    return table[dest]

def expert_ffn(items):
    tokens, gate_w, up_w, down_w = items
    gate = jnp.dot(tokens, gate_w, preferred_element_type=jnp.float32)
    upval = jnp.dot(tokens, up_w, preferred_element_type=jnp.float32)
    act = (jax.nn.silu(gate) * upval).astype(jnp.bfloat16)
    return jnp.dot(act, down_w, preferred_element_type=jnp.float32).astype(jnp.bfloat16)

def reference(x_in, routes, conv_state, ssm_state, mamba_gain, in_x, in_z, conv_w, conv_b, xproj_dt, xproj_bc, dt_proj, dt_bias, a_rate, d_skip, out_proj, moe_gain, router, w_gate, w_up, w_down):
    normed = rms_norm(x_in, mamba_gain)
    u_pre = jnp.dot(normed, in_x, preferred_element_type=jnp.float32)
    z_gate = jnp.dot(normed, in_z, preferred_element_type=jnp.float32)
    requests = u_pre.shape[0] // DRAFT
    seq = jnp.concatenate([conv_state, u_pre.reshape(requests, DRAFT, CH)], axis=1)
    conv = jnp.zeros((requests, DRAFT, CH), jnp.float32) + conv_b
    for tap in range(4):
        conv = conv + conv_w[tap] * seq[:, tap:tap + DRAFT]
    u_act = jax.nn.silu(conv).astype(jnp.bfloat16)
    flat_u = u_act.reshape(-1, CH)
    dt_low = jnp.dot(flat_u, xproj_dt, preferred_element_type=jnp.float32)
    maps = jnp.dot(flat_u, xproj_bc, preferred_element_type=jnp.float32)
    steps = jax.nn.softplus(jnp.dot(dt_low.astype(jnp.bfloat16), dt_proj, preferred_element_type=jnp.float32) + dt_bias)
    b_maps = maps[:, :N].reshape(requests, DRAFT, N)
    c_maps = maps[:, N:].reshape(requests, DRAFT, N)
    outputs, new_state = ssm_steps(u_act.astype(jnp.float32), steps.reshape(requests, DRAFT, CH), b_maps, c_maps, ssm_state, a_rate, d_skip)
    gated = (outputs.reshape(-1, CH) * jax.nn.silu(z_gate)).astype(jnp.bfloat16)
    mixed = jnp.dot(gated, out_proj, preferred_element_type=jnp.float32)
    stream = (x_in.astype(jnp.float32) + mixed).astype(jnp.bfloat16)
    normed2 = rms_norm(stream, moe_gain)
    logits = jnp.dot(normed2, router, preferred_element_type=jnp.float32)
    all_labels = jnp.arange(EXPERTS_ALL, dtype=jnp.int32)
    pick = (routes[:, :, None] == all_labels).astype(jnp.float32)
    chosen = lax.optimization_barrier(jnp.sum(logits[:, None, :] * pick, axis=-1))
    weight0 = jax.nn.sigmoid(chosen[:, 0] - chosen[:, 1])
    blocks = N_EXPERT
    labels = jnp.arange(EXPERTS, dtype=jnp.int32)
    flat_routes = routes.reshape(blocks, TOPK * TOK_DEV)
    onehot = (flat_routes[..., None] == labels).astype(jnp.int32)
    rank = jnp.cumsum(onehot, axis=1) - 1
    slot = lax.optimization_barrier(jnp.sum(rank * onehot, axis=-1))
    inside = lax.optimization_barrier(jnp.sum(onehot, axis=-1))
    dest = jnp.where(inside > 0, flat_routes * CAP + slot, EXPERTS * CAP).astype(jnp.int32)
    rows = jnp.repeat(normed2, TOPK, axis=0).reshape(blocks, TOPK * TOK_DEV, D)
    buffer = jax.vmap(place_rows)(dest, rows)
    per_expert = buffer.reshape(blocks, EXPERTS, CAP, D).transpose(1, 0, 2, 3).reshape(EXPERTS, blocks * CAP, D)
    gate_w = w_gate.reshape(D, EXPERTS, HID).transpose(1, 0, 2)
    up_w = w_up.reshape(D, EXPERTS, HID).transpose(1, 0, 2)
    down_w = w_down.reshape(EXPERTS, HID, D)
    results = lax.map(expert_ffn, (per_expert, gate_w, up_w, down_w))
    back = results.reshape(EXPERTS, blocks, CAP, D).transpose(1, 0, 2, 3).reshape(blocks, EXPERTS * CAP, D)
    back = jnp.concatenate([back, jnp.zeros((blocks, 1, D), jnp.bfloat16)], axis=1)
    picked = jax.vmap(take_rows)(back, dest).reshape(-1, TOPK, D).astype(jnp.float32)
    total = stream.astype(jnp.float32) + weight0[:, None] * picked[:, 0] + (1.0 - weight0)[:, None] * picked[:, 1]
    return (total.astype(jnp.bfloat16), new_state)
```

```python
import jax
import jax.numpy as jnp
import numpy as np
from jax import lax
from jax.sharding import PartitionSpec as P

EXPERTS = 2
DRAFT = 8
CAP = 16
F32 = jnp.float32
BF16 = jnp.bfloat16


def ring_order(owners):
    if owners == 8:
        return [0, 2, 4, 6, 7, 5, 3, 1]
    return list(range(owners))


def ring_tables(owners):
    order = ring_order(owners)
    place = {dev: i for i, dev in enumerate(order)}
    half = owners // 2
    ahead = np.zeros((owners, 2, owners), np.int32)
    for p in range(owners):
        for c in range(2):
            step = 1 if c == 0 else -1
            for d in range(owners):
                ahead[p, c, d] = order[(place[p] + step * d) % owners]
    perm = []
    for p in range(owners):
        for c in range(2):
            perm.append((p * 2 + c, int(ahead[p, c, 1]) * 2 + c))
    return ahead, perm, half


def over_cuts(value):
    return lax.ppermute(value, "cuts", [(0, 1), (1, 0)])


def over_expert(value, flip, owners):
    return lax.ppermute(value, "expert", [(i, i ^ flip) for i in range(owners)])


def rms_norm(values, gain):
    values = values.astype(F32)
    scale = lax.rsqrt(jnp.mean(values * values, axis=-1, keepdims=True) + 1e-05)
    return (values * scale * gain).astype(BF16)


def ssm_steps(inputs, steps, b_maps, c_maps, state, a_rate, d_skip):
    outputs = []
    for place in range(inputs.shape[1]):
        decay = jnp.exp(-steps[:, place, None, :] * a_rate[None])
        state = (
            decay * state
            + (steps[:, place] * inputs[:, place])[:, None, :] * b_maps[:, place, :, None]
        )
        outputs.append(
            jnp.sum(c_maps[:, place, :, None] * state, axis=1) + d_skip * inputs[:, place]
        )
    return (jnp.stack(outputs, axis=1), state)


def halves(first, second, core):
    return jnp.concatenate(
        [jnp.where(core == 0, first, second), jnp.where(core == 0, second, first)], axis=-1
    )


def gather_tokens(x_in, owners, core, ahead, perm):
    half = owners // 2
    rows, width = x_in.shape

    def send(value):
        return lax.ppermute(value, ("expert", "cuts"), perm)

    other = over_cuts(x_in)
    part_a, part_b = [x_in], [other]
    for step in range(1, half + 1):
        part_a.append(send(part_a[-1]))
        if step < half:
            part_b.append(send(part_b[-1]))
    mine = [halves(part_a[d], part_b[d], core) for d in range(half)]
    stack = jnp.concatenate(mine[1:], axis=0)
    theirs = over_cuts(stack).reshape(half - 1, rows, 2 * width)
    far = halves(part_a[half], over_cuts(part_a[half]), core)
    out = jnp.zeros((owners * rows, 2 * width), x_in.dtype)

    def put(buffer, block, index):
        return lax.dynamic_update_slice(buffer, block, (index * rows, 0))

    out = put(out, mine[0], ahead[core, 0])
    for d in range(1, half):
        out = put(out, mine[d], ahead[1 - core, d])
        out = put(out, theirs[d - 1], ahead[core, d])
    return put(out, far, ahead[core, half])


def sum_all(part, owners, expert, core):
    def split(value, bit):
        size = value.shape[0] // 2
        return (
            lax.dynamic_slice_in_dim(value, bit * size, size, 0),
            lax.dynamic_slice_in_dim(value, (1 - bit) * size, size, 0),
        )

    def join(mine, theirs, bit):
        size = mine.shape[0]
        out = jnp.zeros((2 * size,) + mine.shape[1:], mine.dtype)
        out = lax.dynamic_update_slice_in_dim(out, mine, bit * size, 0)
        return lax.dynamic_update_slice_in_dim(out, theirs, (1 - bit) * size, 0)

    keep, give = split(part, core)
    keep = keep + over_cuts(give.astype(BF16)).astype(F32)
    low = expert % 2
    keep, give = split(keep, low)
    keep = keep + over_expert(give.astype(BF16), 1, owners).astype(F32)
    flip = 2
    while flip < owners:
        keep = keep + over_expert(keep.astype(BF16), flip, owners).astype(F32)
        flip *= 2
    keep = keep.astype(BF16)
    keep = join(keep, over_expert(keep, 1, owners), low)
    return join(keep, over_cuts(keep), core)


def scatter_sum(term, rows, owners, core, ahead, perm):
    half = owners // 2
    width = term.shape[1] // 2
    here = core * width
    there = (1 - core) * width

    def block(index, start, size):
        return lax.dynamic_slice(term, (index * rows, start), (rows, size))

    def send(value):
        return lax.ppermute(value.astype(BF16), ("expert", "cuts"), perm)

    give = jnp.concatenate(
        [block(ahead[1 - core, d], start, width) for d in range(1, half) for start in (here, there)]
        + [block(ahead[core, half], there, width), block(ahead[core, 0], there, width)],
        axis=0,
    ).astype(BF16)
    got = over_cuts(give).astype(F32).reshape(2 * half, rows, width)
    acc_a = block(ahead[core, half], here, width) + got[2 * half - 2]
    acc_a = send(acc_a).astype(F32)
    acc_b = None
    for d in range(half - 1, 0, -1):
        local_a = block(ahead[core, d], here, width) + got[2 * d - 1]
        local_b = block(ahead[core, d], there, width) + got[2 * d - 2]
        acc_a = send(acc_a + local_a).astype(F32)
        acc_b = send(local_b if acc_b is None else acc_b + local_b).astype(F32)
    cross = over_cuts(acc_b.astype(BF16)).astype(F32)
    return block(ahead[core, 0], here, width) + got[2 * half - 1] + acc_a + cross


def on_device(
    x_in,
    routes,
    conv_state,
    ssm_state,
    mamba_gain,
    in_x,
    in_z,
    conv_w,
    conv_b,
    xproj_dt,
    xproj_bc,
    dt_proj,
    dt_bias,
    a_rate,
    d_skip,
    out_proj,
    moe_gain,
    router,
    w_gate,
    w_up,
    w_down,
):
    tok_count, half_width = x_in.shape
    requests = conv_state.shape[0]
    channels = in_x.shape[1]
    states = a_rate.shape[0]
    topk = routes.shape[1]
    owners = lax.axis_size("expert")
    expert = lax.axis_index("expert")
    core = lax.axis_index("cuts")
    table, perm, half = ring_tables(owners)
    ahead = lax.dynamic_index_in_dim(jnp.asarray(table), expert, 0, keepdims=False)
    full_x = gather_tokens(x_in, owners, core, ahead, perm)
    normed = rms_norm(full_x, mamba_gain)
    u_pre = jnp.dot(normed, in_x, preferred_element_type=F32)
    z_gate = jnp.dot(normed, in_z, preferred_element_type=F32)
    seq = jnp.concatenate([conv_state, u_pre.reshape(requests, DRAFT, channels)], axis=1)
    conv = jnp.zeros((requests, DRAFT, channels), F32) + conv_b
    for tap in range(conv_w.shape[0]):
        conv = conv + conv_w[tap] * seq[:, tap : tap + DRAFT]
    u_act = jax.nn.silu(conv).astype(BF16)
    flat_u = u_act.reshape(requests * DRAFT, channels)
    rank = xproj_dt.shape[1]
    part = jnp.concatenate(
        [
            jnp.dot(flat_u, xproj_dt, preferred_element_type=F32),
            jnp.dot(flat_u, xproj_bc, preferred_element_type=F32),
        ],
        axis=1,
    )
    total = sum_all(part, owners, expert, core)
    dt_low = total[:, :rank]
    maps = total[:, rank:].astype(F32)
    steps = jax.nn.softplus(jnp.dot(dt_low, dt_proj, preferred_element_type=F32) + dt_bias)
    b_maps = maps[:, :states].reshape(requests, DRAFT, states)
    c_maps = maps[:, states:].reshape(requests, DRAFT, states)
    outputs, new_state = ssm_steps(
        u_act.astype(F32),
        steps.reshape(requests, DRAFT, channels),
        b_maps,
        c_maps,
        ssm_state,
        a_rate,
        d_skip,
    )
    gated = (outputs.reshape(requests * DRAFT, channels) * jax.nn.silu(z_gate)).astype(BF16)
    term = jnp.dot(gated, out_proj, preferred_element_type=F32)
    mixed_half = scatter_sum(term, tok_count, owners, core, ahead, perm)
    stream_half = (x_in.astype(F32) + mixed_half).astype(BF16)

    labels = jnp.arange(EXPERTS, dtype=jnp.int32)
    named = jnp.any(routes[:, :, None] == labels, axis=1).astype(BF16)
    earlier = (jnp.arange(tok_count)[:, None] > jnp.arange(tok_count)[None, :]).astype(BF16)
    slot = jnp.dot(earlier, named, preferred_element_type=F32)
    rows = jnp.arange(CAP, dtype=F32)
    pick = ((slot.T[:, None, :] == rows[None, :, None]) & (named.T[:, None, :] > 0)).astype(BF16)
    buffer = (
        jnp.dot(pick.reshape(EXPERTS * CAP, tok_count), stream_half, preferred_element_type=F32)
        .astype(BF16)
        .reshape(EXPERTS, CAP, half_width)
    )
    holders = owners // EXPERTS
    own = expert // holders

    def exchange(value, flip):
        return over_expert(value, flip, owners)

    kept = lax.dynamic_index_in_dim(buffer, own, 0, keepdims=False)
    given = lax.dynamic_index_in_dim(buffer, 1 - own, 0, keepdims=False)
    pair = jnp.concatenate([kept, exchange(given, holders)], axis=0)
    pieces = [pair] + [exchange(pair, flip) for flip in range(1, holders)]
    tokens_half = jnp.concatenate(pieces, axis=0)
    tokens = halves(tokens_half, over_cuts(tokens_half), core)
    normed2 = rms_norm(tokens, moe_gain)
    gate = jnp.dot(normed2, w_gate, preferred_element_type=F32)
    upval = jnp.dot(normed2, w_up, preferred_element_type=F32)
    act = (jax.nn.silu(gate) * upval).astype(BF16)
    partial_out = jnp.dot(act, w_down, preferred_element_type=F32)
    count = partial_out.shape[0]
    mine = lax.dynamic_slice(partial_out, (0, core * half_width), (count, half_width))
    theirs = lax.dynamic_slice(partial_out, (0, (1 - core) * half_width), (count, half_width))
    summed = mine + over_cuts(theirs.astype(BF16)).astype(F32)
    summed = summed.reshape(holders, 2 * CAP, half_width)
    result = summed[0]
    for flip in range(1, holders):
        result = result + exchange(summed[flip].astype(BF16), flip).astype(F32)
    result = result.astype(BF16)
    back = exchange(result[CAP:], holders)

    stream = halves(stream_half, over_cuts(stream_half), core)
    logits = jnp.dot(rms_norm(stream, moe_gain), router, preferred_element_type=F32)
    all_labels = jnp.arange(router.shape[1], dtype=jnp.int32)
    which = (routes[:, :, None] == all_labels).astype(F32)
    chosen = jnp.sum(logits[:, None, :] * which, axis=-1)
    weight0 = jax.nn.sigmoid(chosen[:, 0] - chosen[:, 1])
    weights = jnp.stack([weight0, 1.0 - weight0], axis=1)
    weight = jnp.sum(jnp.where(routes < EXPERTS, weights, 0.0), axis=1)
    table = jnp.concatenate([result[:CAP], back], axis=0)
    pick_own = jnp.where(own == 0, pick, pick[::-1]).reshape(EXPERTS * CAP, tok_count)
    expert_out = lax.dot_general(
        pick_own, table, (((0,), (0,)), ((), ())), preferred_element_type=F32
    )
    out = stream_half.astype(F32) + weight[:, None] * expert_out
    return (out.astype(BF16), new_state)


def solution(mesh):
    return jax.shard_map(
        on_device,
        mesh=mesh,
        in_specs=(
            P(("group", "expert"), "cuts"),
            P(("group", "expert"), None),
            P("group", None, ("expert", "cuts")),
            P("group", None, ("expert", "cuts")),
            P(),
            P(None, ("expert", "cuts")),
            P(None, ("expert", "cuts")),
            P(None, ("expert", "cuts")),
            P(("expert", "cuts")),
            P(("expert", "cuts"), None),
            P(("expert", "cuts"), None),
            P(None, ("expert", "cuts")),
            P(("expert", "cuts")),
            P(None, ("expert", "cuts")),
            P(("expert", "cuts")),
            P(("expert", "cuts"), None),
            P(),
            P(),
            P(None, ("expert", "cuts")),
            P(None, ("expert", "cuts")),
            P(("expert", "cuts"), None),
        ),
        out_specs=(P(("group", "expert"), "cuts"), P("group", None, ("expert", "cuts"))),
        check_vma=False,
    )
```

```python
import functools

import jax
import jax.numpy as jnp
from jax import lax
from jax.experimental import pallas as pl
from jax.experimental.pallas import tpu as pltpu
from jax.sharding import PartitionSpec as P

EXPERTS = 2
DRAFT = 8
CAP = 16
F32 = jnp.float32
BF16 = jnp.bfloat16


def ring_place(index, owners):
    if owners == 8:
        low = index % 2
        return index // 2 * (1 - 2 * low) + 7 * low
    return index


def ring_index(place, owners):
    if owners == 8:
        low = place // 4
        return 2 * place * (1 - 2 * low) + 15 * low
    return place


def ring_perm(owners):
    pairs = []
    for index in range(owners):
        for core in range(2):
            to = ring_index((ring_place(index, owners) + 1 - 2 * core) % owners, owners)
            pairs.append((2 * index + core, 2 * to + core))
    return pairs


def ring_ahead(expert, core, owners):
    place = ring_place(expert, owners)
    return [
        ring_index(lax.rem(place + (1 - 2 * core) * d + owners, owners), owners)
        for d in range(owners // 2 + 1)
    ]


def over_cuts(value):
    return lax.ppermute(value, "cuts", [(0, 1), (1, 0)])


def over_expert(value, flip, owners):
    return lax.ppermute(value, "expert", [(i, i ^ flip) for i in range(owners)])


def rms_norm(values, gain):
    values = values.astype(F32)
    scale = lax.rsqrt(jnp.mean(values * values, axis=-1, keepdims=True) + 1e-05)
    return (values * scale * gain).astype(BF16)


def ssm_steps(inputs, steps, b_maps, c_maps, state, a_rate, d_skip):
    outputs = []
    for place in range(inputs.shape[1]):
        decay = jnp.exp(-steps[:, place, None, :] * a_rate[None])
        state = (
            decay * state
            + (steps[:, place] * inputs[:, place])[:, None, :] * b_maps[:, place, :, None]
        )
        outputs.append(
            jnp.sum(c_maps[:, place, :, None] * state, axis=1) + d_skip * inputs[:, place]
        )
    return (jnp.stack(outputs, axis=1), state)


def halves(first, second, core):
    return jnp.concatenate(
        [jnp.where(core == 0, first, second), jnp.where(core == 0, second, first)], axis=-1
    )


def gather_tokens(x_in, owners, core, ahead, behind, perm):
    half = owners // 2
    rows, width = x_in.shape

    def send(value):
        return lax.ppermute(value, ("expert", "cuts"), perm)

    other = over_cuts(x_in)
    part_a, part_b = [x_in], [other]
    for step in range(1, half + 1):
        part_a.append(send(part_a[-1]))
        if step < half:
            part_b.append(send(part_b[-1]))
    mine = [halves(part_a[d], part_b[d], core) for d in range(half)]
    stack = jnp.concatenate(mine[1:], axis=0)
    theirs = over_cuts(stack).reshape(half - 1, rows, 2 * width)
    far = halves(part_a[half], over_cuts(part_a[half]), core)
    out = jnp.zeros((owners * rows, 2 * width), x_in.dtype)

    def put(buffer, block, index):
        return lax.dynamic_update_slice(buffer, block, (index * rows, 0))

    out = put(out, mine[0], ahead[0])
    for d in range(1, half):
        out = put(out, mine[d], behind[d])
        out = put(out, theirs[d - 1], ahead[d])
    return put(out, far, ahead[half])


def sum_all(part, owners, expert, core):
    def split(value, bit):
        size = value.shape[0] // 2
        return (
            lax.dynamic_slice_in_dim(value, bit * size, size, 0),
            lax.dynamic_slice_in_dim(value, (1 - bit) * size, size, 0),
        )

    def join(mine, theirs, bit):
        size = mine.shape[0]
        out = jnp.zeros((2 * size,) + mine.shape[1:], mine.dtype)
        out = lax.dynamic_update_slice_in_dim(out, mine, bit * size, 0)
        return lax.dynamic_update_slice_in_dim(out, theirs, (1 - bit) * size, 0)

    keep, give = split(part, core)
    keep = keep + over_cuts(give.astype(BF16)).astype(F32)
    low = expert % 2
    keep, give = split(keep, low)
    keep = keep + over_expert(give.astype(BF16), 1, owners).astype(F32)
    flip = 2
    while flip < owners:
        keep = keep + over_expert(keep.astype(BF16), flip, owners).astype(F32)
        flip *= 2
    keep = keep.astype(BF16)
    keep = join(keep, over_expert(keep, 1, owners), low)
    return join(keep, over_cuts(keep), core)


def project_kernel(half, rows, width, place_ref, g_ref, h_ref, wg_ref, wh_ref, near_ref, far_ref, own_ref, other_ref):
    core = place_ref[half + 1]
    here = pl.multiple_of(core * width, 128)
    there = pl.multiple_of((1 - core) * width, 128)
    picked = [pl.ds(pl.multiple_of(place_ref[d] * rows, rows), rows) for d in range(half + 1)]
    lhs_g = jnp.concatenate([g_ref[at, :] for at in picked], axis=0)
    lhs_h = jnp.concatenate([h_ref[at, :] for at in picked], axis=0)
    tile = 512
    for start in range(0, width, tile):
        at = pl.ds(here + start, tile)
        term = jnp.dot(lhs_g, wg_ref[:, at], preferred_element_type=F32) + jnp.dot(
            lhs_h, wh_ref[:, at], preferred_element_type=F32
        )
        own_ref[:, start : start + tile] = term[:rows]
        near_ref[:, start : start + tile] = term[rows : half * rows]
        far_ref[:, start : start + tile] = term[half * rows :].astype(BF16)
        at = pl.ds(there + start, tile)
        term = jnp.dot(
            lhs_g[rows : half * rows], wg_ref[:, at], preferred_element_type=F32
        ) + jnp.dot(lhs_h[rows : half * rows], wh_ref[:, at], preferred_element_type=F32)
        other_ref[:, start : start + tile] = term


def project_blocks(gated, gated_other, out_proj, out_other, rows, half, places):
    width = out_proj.shape[1] // 2
    vmem = pl.BlockSpec(memory_space=pltpu.VMEM)
    return pl.pallas_call(
        functools.partial(project_kernel, half, rows, width),
        out_shape=(
            jax.ShapeDtypeStruct(((half - 1) * rows, width), F32),
            jax.ShapeDtypeStruct((rows, width), BF16),
            jax.ShapeDtypeStruct((rows, width), F32),
            jax.ShapeDtypeStruct(((half - 1) * rows, width), F32),
        ),
        in_specs=[pl.BlockSpec(memory_space=pltpu.SMEM)] + [vmem] * 4,
        out_specs=[vmem] * 4,
        compiler_params=pltpu.CompilerParams(vmem_limit_bytes=40 << 20),
        name="project",
    )(places, gated, gated_other, out_proj, out_other)


def scatter_sum(near, far, own, other, rows, owners, perm):
    half = owners // 2

    def send(value):
        return lax.ppermute(value.astype(BF16), ("expert", "cuts"), perm)

    acc_a = send(far)
    acc_b = None
    for d in range(half - 1, 0, -1):
        at = slice((d - 1) * rows, d * rows)
        acc_a = send(acc_a.astype(F32) + near[at])
        acc_b = send(other[at] if acc_b is None else acc_b.astype(F32) + other[at])
    return own + acc_a.astype(F32) + over_cuts(acc_b).astype(F32)


def experts_kernel(tiles, x_ref, gain_ref, wg_hbm, wu_hbm, wd_hbm, out_ref, wg, wu, wd, sems):
    tile = wg.shape[2]
    copies = []
    for i in range(tiles):
        at = pl.ds(i * tile, tile)
        copies.append(
            (
                pltpu.make_async_copy(wg_hbm.at[:, at], wg.at[i], sems.at[0, i]),
                pltpu.make_async_copy(wu_hbm.at[:, at], wu.at[i], sems.at[1, i]),
                pltpu.make_async_copy(wd_hbm.at[at, :], wd.at[i], sems.at[2, i]),
            )
        )
    for group in copies:
        for copy in group:
            copy.start()
    values = x_ref[...].astype(F32)
    scale = lax.rsqrt(jnp.mean(values * values, axis=-1, keepdims=True) + 1e-05)
    x = (values * scale * gain_ref[...]).astype(BF16)
    for i in range(tiles):
        copies[i][0].wait()
        gate = jnp.dot(x, wg[i], preferred_element_type=F32)
        copies[i][1].wait()
        upval = jnp.dot(x, wu[i], preferred_element_type=F32)
        act = (gate * jax.nn.sigmoid(gate) * upval).astype(BF16)
        copies[i][2].wait()
        term = jnp.dot(act, wd[i], preferred_element_type=F32)
        if i == 0:
            out_ref[...] = term
        else:
            out_ref[...] += term


def run_experts(tokens, gain, w_gate, w_up, w_down):
    count, width = tokens.shape
    hidden = w_gate.shape[1]
    tile = 256
    tiles = hidden // tile
    vmem = pl.BlockSpec(memory_space=pltpu.VMEM)
    hbm = pl.BlockSpec(memory_space=pltpu.HBM)
    return pl.pallas_call(
        functools.partial(experts_kernel, tiles),
        out_shape=jax.ShapeDtypeStruct((count, width), F32),
        in_specs=[vmem, vmem, hbm, hbm, hbm],
        out_specs=vmem,
        scratch_shapes=[
            pltpu.VMEM((tiles, width, tile), BF16),
            pltpu.VMEM((tiles, width, tile), BF16),
            pltpu.VMEM((tiles, tile, width), BF16),
            pltpu.SemaphoreType.DMA((3, tiles)),
        ],
        compiler_params=pltpu.CompilerParams(vmem_limit_bytes=48 << 20),
        name="experts",
    )(tokens, gain.reshape(1, width), w_gate, w_up, w_down)


def on_device(
    x_in,
    routes,
    conv_state,
    ssm_state,
    mamba_gain,
    in_x,
    in_z,
    conv_w,
    conv_b,
    xproj_dt,
    xproj_bc,
    dt_proj,
    dt_bias,
    a_rate,
    d_skip,
    out_proj,
    moe_gain,
    router,
    w_gate,
    w_up,
    w_down,
):
    tok_count, half_width = x_in.shape
    requests = conv_state.shape[0]
    channels = in_x.shape[1]
    states = a_rate.shape[0]
    topk = routes.shape[1]
    owners = lax.axis_size("expert")
    expert = lax.axis_index("expert")
    core = lax.axis_index("cuts")
    half = owners // 2
    perm = ring_perm(owners)
    ahead = ring_ahead(expert, core, owners)
    behind = ring_ahead(expert, 1 - core, owners)
    out_other = over_cuts(out_proj)
    full_x = gather_tokens(x_in, owners, core, ahead, behind, perm)
    normed = rms_norm(full_x, mamba_gain)
    u_pre = jnp.dot(normed, in_x, preferred_element_type=F32)
    z_gate = jnp.dot(normed, in_z, preferred_element_type=F32)
    seq = jnp.concatenate([conv_state, u_pre.reshape(requests, DRAFT, channels)], axis=1)
    conv = jnp.zeros((requests, DRAFT, channels), F32) + conv_b
    for tap in range(conv_w.shape[0]):
        conv = conv + conv_w[tap] * seq[:, tap : tap + DRAFT]
    u_act = jax.nn.silu(conv).astype(BF16)
    flat_u = u_act.reshape(requests * DRAFT, channels)
    rank = xproj_dt.shape[1]
    part = jnp.concatenate(
        [
            jnp.dot(flat_u, xproj_dt, preferred_element_type=F32),
            jnp.dot(flat_u, xproj_bc, preferred_element_type=F32),
        ],
        axis=1,
    )
    total = sum_all(part, owners, expert, core)
    dt_low = total[:, :rank]
    maps = total[:, rank:].astype(F32)
    steps = jax.nn.softplus(jnp.dot(dt_low, dt_proj, preferred_element_type=F32) + dt_bias)
    b_maps = maps[:, :states].reshape(requests, DRAFT, states)
    c_maps = maps[:, states:].reshape(requests, DRAFT, states)
    outputs, new_state = ssm_steps(
        u_act.astype(F32),
        steps.reshape(requests, DRAFT, channels),
        b_maps,
        c_maps,
        ssm_state,
        a_rate,
        d_skip,
    )
    gated = (outputs.reshape(requests * DRAFT, channels) * jax.nn.silu(z_gate)).astype(BF16)
    near, far, own_term, other = project_blocks(
        gated,
        over_cuts(gated),
        out_proj,
        out_other,
        tok_count,
        half,
        jnp.stack(ahead + [core]).astype(jnp.int32),
    )
    mixed_half = scatter_sum(near, far, own_term, other, tok_count, owners, perm)
    stream_half = (x_in.astype(F32) + mixed_half).astype(BF16)

    labels = jnp.arange(EXPERTS, dtype=jnp.int32)
    named = jnp.any(routes[:, :, None] == labels, axis=1).astype(BF16)
    earlier = (jnp.arange(tok_count)[:, None] > jnp.arange(tok_count)[None, :]).astype(BF16)
    slot = jnp.dot(earlier, named, preferred_element_type=F32)
    rows = jnp.arange(CAP, dtype=F32)
    pick = ((slot.T[:, None, :] == rows[None, :, None]) & (named.T[:, None, :] > 0)).astype(BF16)
    buffer = (
        jnp.dot(pick.reshape(EXPERTS * CAP, tok_count), stream_half, preferred_element_type=F32)
        .astype(BF16)
        .reshape(EXPERTS, CAP, half_width)
    )
    holders = owners // EXPERTS
    own = expert // holders

    def exchange(value, flip):
        return over_expert(value, flip, owners)

    kept = lax.dynamic_index_in_dim(buffer, own, 0, keepdims=False)
    given = lax.dynamic_index_in_dim(buffer, 1 - own, 0, keepdims=False)
    pair = jnp.concatenate([kept, exchange(given, holders)], axis=0)
    pieces = [pair] + [exchange(pair, flip) for flip in range(1, holders)]
    tokens_half = jnp.concatenate(pieces, axis=0)
    tokens = halves(tokens_half, over_cuts(tokens_half), core)
    partial_out = run_experts(tokens, moe_gain, w_gate, w_up, w_down)
    count = partial_out.shape[0]
    mine = lax.dynamic_slice(partial_out, (0, core * half_width), (count, half_width))
    theirs = lax.dynamic_slice(partial_out, (0, (1 - core) * half_width), (count, half_width))
    summed = mine + over_cuts(theirs.astype(BF16)).astype(F32)
    summed = summed.reshape(holders, 2 * CAP, half_width)
    result = summed[0]
    for flip in range(1, holders):
        result = result + exchange(summed[flip].astype(BF16), flip).astype(F32)
    result = result.astype(BF16)
    back = exchange(result[CAP:], holders)

    stream = halves(stream_half, over_cuts(stream_half), core)
    logits = jnp.dot(rms_norm(stream, moe_gain), router, preferred_element_type=F32)
    all_labels = jnp.arange(router.shape[1], dtype=jnp.int32)
    which = (routes[:, :, None] == all_labels).astype(F32)
    chosen = jnp.sum(logits[:, None, :] * which, axis=-1)
    weight0 = jax.nn.sigmoid(chosen[:, 0] - chosen[:, 1])
    weights = jnp.stack([weight0, 1.0 - weight0], axis=1)
    weight = jnp.sum(jnp.where(routes < EXPERTS, weights, 0.0), axis=1)
    table = jnp.concatenate([result[:CAP], back], axis=0)
    pick_own = jnp.where(own == 0, pick, pick[::-1]).reshape(EXPERTS * CAP, tok_count)
    expert_out = lax.dot_general(
        pick_own, table, (((0,), (0,)), ((), ())), preferred_element_type=F32
    )
    out = stream_half.astype(F32) + weight[:, None] * expert_out
    return (out.astype(BF16), new_state)


def solution(mesh):
    return jax.shard_map(
        on_device,
        mesh=mesh,
        in_specs=(
            P(("group", "expert"), "cuts"),
            P(("group", "expert"), None),
            P("group", None, ("expert", "cuts")),
            P("group", None, ("expert", "cuts")),
            P(),
            P(None, ("expert", "cuts")),
            P(None, ("expert", "cuts")),
            P(None, ("expert", "cuts")),
            P(("expert", "cuts")),
            P(("expert", "cuts"), None),
            P(("expert", "cuts"), None),
            P(None, ("expert", "cuts")),
            P(("expert", "cuts")),
            P(None, ("expert", "cuts")),
            P(("expert", "cuts")),
            P(("expert", "cuts"), None),
            P(),
            P(),
            P(None, ("expert", "cuts")),
            P(None, ("expert", "cuts")),
            P(("expert", "cuts"), None),
        ),
        out_specs=(P(("group", "expert"), "cuts"), P("group", None, ("expert", "cuts"))),
        check_vma=False,
    )
```

```python
import functools

import jax
import jax.numpy as jnp
from jax import lax
from jax.experimental import pallas as pl
from jax.experimental.pallas import tpu as pltpu
from jax.sharding import PartitionSpec as P

EXPERTS = 2
DRAFT = 8
CAP = 16
F32 = jnp.float32
BF16 = jnp.bfloat16
VMEM_LIMIT = 28 << 20


def ring_place(index, owners):
    if owners == 8:
        low = index % 2
        return index // 2 * (1 - 2 * low) + 7 * low
    return index


def ring_index(place, owners):
    if owners == 8:
        low = place // 4
        return 2 * place * (1 - 2 * low) + 15 * low
    return place


def ring_perm(owners):
    pairs = []
    for index in range(owners):
        for core in range(2):
            to = ring_index((ring_place(index, owners) + 1 - 2 * core) % owners, owners)
            pairs.append((2 * index + core, 2 * to + core))
    return pairs


def ring_ahead(expert, core, owners):
    place = ring_place(expert, owners)
    return [
        ring_index(lax.rem(place + (1 - 2 * core) * d + owners, owners), owners)
        for d in range(owners // 2 + 1)
    ]


def over_cuts(value):
    return lax.ppermute(value, "cuts", [(0, 1), (1, 0)])


def over_expert(value, flip, owners):
    return lax.ppermute(value, "expert", [(i, i ^ flip) for i in range(owners)])


def rms_norm(values, gain):
    values = values.astype(F32)
    scale = lax.rsqrt(jnp.mean(values * values, axis=-1, keepdims=True) + 1e-05)
    return (values * scale * gain).astype(BF16)


def halves(first, second, core):
    return jnp.concatenate(
        [jnp.where(core == 0, first, second), jnp.where(core == 0, second, first)], axis=-1
    )


def gather_tokens(x_in, owners, core, ahead, behind, perm):
    half = owners // 2
    rows, width = x_in.shape

    def send(value):
        return lax.ppermute(value, ("expert", "cuts"), perm)

    other = over_cuts(x_in)
    part_a, part_b = [x_in], [other]
    for step in range(1, half + 1):
        part_a.append(send(part_a[-1]))
        if step < half:
            part_b.append(send(part_b[-1]))
    part_b, near = lax.optimization_barrier((part_b, part_a[:half]))
    part_a = [*near, part_a[half]]
    mine = [halves(part_a[d], part_b[d], core) for d in range(half)]
    stack = jnp.concatenate(mine[1:], axis=0)
    theirs = over_cuts(stack).reshape(half - 1, rows, 2 * width)
    far = halves(part_a[half], over_cuts(part_a[half]), core)
    out = jnp.zeros((owners * rows, 2 * width), x_in.dtype)

    def put(buffer, block, index):
        return lax.dynamic_update_slice(buffer, block, (index * rows, 0))

    out = put(out, mine[0], ahead[0])
    for d in range(1, half):
        out = put(out, mine[d], behind[d])
        out = put(out, theirs[d - 1], ahead[d])
    return put(out, far, ahead[half])


def sum_all(part, owners, expert, core, under):
    done = []

    def beside(value):
        if not under:
            return value
        value, extra = lax.optimization_barrier((value, under.pop(0)()))
        done.append(extra)
        return value

    def split(value, bit):
        size = value.shape[0] // 2
        return (
            lax.dynamic_slice_in_dim(value, bit * size, size, 0),
            lax.dynamic_slice_in_dim(value, (1 - bit) * size, size, 0),
        )

    def join(mine, theirs, bit):
        size = mine.shape[0]
        out = jnp.zeros((2 * size,) + mine.shape[1:], mine.dtype)
        out = lax.dynamic_update_slice_in_dim(out, mine, bit * size, 0)
        return lax.dynamic_update_slice_in_dim(out, theirs, (1 - bit) * size, 0)

    keep, give = split(part, core)
    keep = keep + over_cuts(give.astype(BF16)).astype(F32)
    low = expert % 2
    keep, give = split(keep, low)
    keep = keep + beside(over_expert(give.astype(BF16), 1, owners)).astype(F32)
    flip = 2
    while flip < owners:
        keep = keep + beside(over_expert(keep.astype(BF16), flip, owners)).astype(F32)
        flip *= 2
    keep = keep.astype(BF16)
    keep = join(keep, beside(over_expert(keep, 1, owners)), low)
    return join(keep, over_cuts(keep), core), done


def scan_kernel(
    total, dt_proj, dt_bias, u_ref, z_ref, state_ref, a_rate, d_skip, gated, new_state, b_all, c_all, dt_all
):
    tokens, channels = u_ref.shape
    states = a_rate.shape[0]
    rank = dt_proj.shape[0]
    raw = jnp.dot(total[:, :rank], dt_proj[...], preferred_element_type=F32) + dt_bias[...]
    dt_all[...] = jnp.maximum(raw, 0.0) + jnp.log1p(jnp.exp(-jnp.abs(raw)))
    ones = jnp.ones((states, channels), BF16)
    diagonal = lax.broadcasted_iota(jnp.int32, (tokens, states, states), 1) == lax.broadcasted_iota(
        jnp.int32, (tokens, states, states), 2
    )
    maps = total[:, rank : rank + 2 * states].astype(F32)
    for start, dest in ((0, b_all), (states, c_all)):
        spread = jnp.broadcast_to(
            maps[:, None, start : start + states], (tokens, states, states)
        )
        spread = jnp.where(diagonal, spread, 0.0).reshape(tokens * states, states).astype(BF16)
        dest[...] = jnp.dot(spread, ones, preferred_element_type=F32)
    rate = -a_rate[...]
    skip = d_skip[...]

    def request(r, carry):
        at = pl.ds(pl.multiple_of(r * DRAFT, DRAFT), DRAFT)
        dt = dt_all[at, :]
        u = u_ref[at, :].astype(F32)
        du = dt * u
        state = state_ref[r]
        out = []
        for p in range(DRAFT):
            spot = pl.ds(pl.multiple_of((r * DRAFT + p) * states, states), states)
            state = jnp.exp(dt[p : p + 1] * rate) * state + du[p : p + 1] * b_all[spot, :]
            out.append(jnp.sum(c_all[spot, :] * state, axis=0, keepdims=True))
        new_state[r] = state
        z = z_ref[at, :]
        y = jnp.concatenate(out, axis=0) + skip * u
        gated[at, :] = y * (z * jax.nn.sigmoid(z))
        return carry

    lax.fori_loop(0, tokens // DRAFT, request, 0, unroll=2)


def scan(total, dt_proj, dt_bias, u, z, ssm_state, a_rate, d_skip):
    tokens, channels = u.shape
    states = a_rate.shape[0]
    vmem = pl.BlockSpec(memory_space=pltpu.VMEM)
    return pl.pallas_call(
        scan_kernel,
        out_shape=(
            jax.ShapeDtypeStruct((tokens, channels), F32),
            jax.ShapeDtypeStruct(ssm_state.shape, F32),
        ),
        in_specs=[vmem] * 8,
        out_specs=[vmem] * 2,
        scratch_shapes=[
            pltpu.VMEM((tokens * states, channels), F32),
            pltpu.VMEM((tokens * states, channels), F32),
            pltpu.VMEM((tokens, channels), F32),
        ],
        compiler_params=pltpu.CompilerParams(vmem_limit_bytes=VMEM_LIMIT),
        name="scan",
    )(
        total,
        dt_proj,
        dt_bias.reshape(1, -1),
        u,
        z,
        ssm_state,
        a_rate,
        d_skip.reshape(1, -1),
    )


def project_kernel(
    half, rows, width, place_ref, id_ref, g_ref, h_ref, wg_ref, wh_ref, near_ref, far_ref, own_ref, other_ref
):
    core = place_ref[half + 1]
    holders = 2 * half // EXPERTS
    ids = id_ref[...]
    column = lax.broadcasted_iota(jnp.int32, (1, (half + 1) * rows), 1)
    target = jnp.zeros_like(column)
    for d in range(half + 1):
        target = jnp.where(column // rows == d, place_ref[d], target)
    picked = (ids == slot_keys(target, column % rows, holders, rows)).astype(F32).astype(BF16)
    here = pl.multiple_of(core * width, 128)
    there = pl.multiple_of((1 - core) * width, 128)
    first = (((0,), (0,)), ((), ()))
    lhs_g = lax.dot_general(picked, g_ref[...], first, preferred_element_type=F32).astype(BF16)
    lhs_h = lax.dot_general(picked, h_ref[...], first, preferred_element_type=F32).astype(BF16)
    tile = 512
    for start in range(0, width, tile):
        at = pl.ds(here + start, tile)
        term = jnp.dot(lhs_g, wg_ref[:, at], preferred_element_type=F32) + jnp.dot(
            lhs_h, wh_ref[:, at], preferred_element_type=F32
        )
        own_ref[:, start : start + tile] = term[:rows]
        near_ref[:, start : start + tile] = term[rows : half * rows]
        far_ref[:, start : start + tile] = term[half * rows :].astype(BF16)
        at = pl.ds(there + start, tile)
        term = jnp.dot(
            lhs_g[rows : half * rows], wg_ref[:, at], preferred_element_type=F32
        ) + jnp.dot(lhs_h[rows : half * rows], wh_ref[:, at], preferred_element_type=F32)
        other_ref[:, start : start + tile] = term


def slots_kernel(routes_ref, out_ref):
    routes = routes_ref[...]
    count = routes.shape[0]
    named = [
        jnp.any(routes == label, axis=1, keepdims=True).astype(F32) for label in range(EXPERTS)
    ]
    idle = 1.0 - named[0] - named[1]
    lane = lax.broadcasted_iota(jnp.int32, (count, 128), 1)
    kinds = jnp.where(lane == 0, named[0], jnp.where(lane == 1, named[1], idle)).astype(BF16)
    earlier = (
        lax.broadcasted_iota(jnp.int32, (count, count), 0)
        > lax.broadcasted_iota(jnp.int32, (count, count), 1)
    )
    ranks = jnp.dot(
        earlier.astype(F32).astype(BF16), kinds, preferred_element_type=F32
    )
    first = jnp.sum(named[0], axis=0, keepdims=True)
    second = jnp.sum(named[1], axis=0, keepdims=True)
    spare = jnp.where(second < CAP, CAP + second, first)
    slot = (
        named[0] * ranks[:, 0:1]
        + named[1] * (CAP + ranks[:, 1:2])
        + idle * (spare + ranks[:, 2:3])
    )
    both = routes.astype(F32)
    out_ref[...] = jnp.concatenate([slot, both], axis=1)


def find_slots(routes):
    vmem = pl.BlockSpec(memory_space=pltpu.VMEM)
    return pl.pallas_call(
        slots_kernel,
        out_shape=jax.ShapeDtypeStruct((routes.shape[0], 1 + routes.shape[1]), F32),
        in_specs=[vmem],
        out_specs=vmem,
        compiler_params=pltpu.CompilerParams(vmem_limit_bytes=1 << 20),
        name="slots",
    )(routes)


def slot_keys(target, row, holders, rows):
    expert = target // holders
    block = jnp.where(row < CAP, target, target + holders * (1 - 2 * expert))
    return block * rows + expert * CAP + row % CAP


def project_blocks(ids, gated, gated_other, out_proj, out_other, rows, half, places):
    width = out_proj.shape[1] // 2
    vmem = pl.BlockSpec(memory_space=pltpu.VMEM)
    return pl.pallas_call(
        functools.partial(project_kernel, half, rows, width),
        out_shape=(
            jax.ShapeDtypeStruct(((half - 1) * rows, width), F32),
            jax.ShapeDtypeStruct((rows, width), BF16),
            jax.ShapeDtypeStruct((rows, width), F32),
            jax.ShapeDtypeStruct(((half - 1) * rows, width), F32),
        ),
        in_specs=[pl.BlockSpec(memory_space=pltpu.SMEM)] + [vmem] * 5,
        out_specs=[vmem] * 4,
        compiler_params=pltpu.CompilerParams(vmem_limit_bytes=VMEM_LIMIT),
        name="project",
    )(places, ids, gated, gated_other, out_proj, out_other)


def scatter_sum(near, far, own, other, rows, owners, perm):
    half = owners // 2

    def send(value):
        return lax.ppermute(value.astype(BF16), ("expert", "cuts"), perm)

    acc_a = send(far)
    acc_b = None
    for d in range(half - 1, 0, -1):
        at = slice((d - 1) * rows, d * rows)
        acc_a = send(acc_a.astype(F32) + near[at])
        acc_b = send(other[at] if acc_b is None else acc_b.astype(F32) + other[at])
    return own + acc_a.astype(F32) + over_cuts(acc_b).astype(F32)


def experts_kernel(tiles, x_ref, gain_ref, wg_hbm, wu_hbm, wd_hbm, out_ref, wg, wu, wd, sems):
    tile = wg.shape[2]
    copies = []
    for i in range(tiles):
        at = pl.ds(i * tile, tile)
        copies.append(
            (
                pltpu.make_async_copy(wg_hbm.at[:, at], wg.at[i], sems.at[0, i]),
                pltpu.make_async_copy(wu_hbm.at[:, at], wu.at[i], sems.at[1, i]),
                pltpu.make_async_copy(wd_hbm.at[at, :], wd.at[i], sems.at[2, i]),
            )
        )
    for group in copies:
        for copy in group:
            copy.start()
    values = x_ref[...].astype(F32)
    scale = lax.rsqrt(jnp.mean(values * values, axis=-1, keepdims=True) + 1e-05)
    x = (values * scale * gain_ref[...]).astype(BF16)
    for i in range(tiles):
        copies[i][0].wait()
        gate = jnp.dot(x, wg[i], preferred_element_type=F32)
        copies[i][1].wait()
        upval = jnp.dot(x, wu[i], preferred_element_type=F32)
        act = (gate * jax.nn.sigmoid(gate) * upval).astype(BF16)
        copies[i][2].wait()
        term = jnp.dot(act, wd[i], preferred_element_type=F32)
        if i == 0:
            out_ref[...] = term
        else:
            out_ref[...] += term


def run_experts(tokens, gain, w_gate, w_up, w_down):
    count, width = tokens.shape
    hidden = w_gate.shape[1]
    tile = 256
    tiles = hidden // tile
    vmem = pl.BlockSpec(memory_space=pltpu.VMEM)
    hbm = pl.BlockSpec(memory_space=pltpu.HBM)
    return pl.pallas_call(
        functools.partial(experts_kernel, tiles),
        out_shape=jax.ShapeDtypeStruct((count, width), F32),
        in_specs=[vmem, vmem, hbm, hbm, hbm],
        out_specs=vmem,
        scratch_shapes=[
            pltpu.VMEM((tiles, width, tile), BF16),
            pltpu.VMEM((tiles, width, tile), BF16),
            pltpu.VMEM((tiles, tile, width), BF16),
            pltpu.SemaphoreType.DMA((3, tiles)),
        ],
        compiler_params=pltpu.CompilerParams(vmem_limit_bytes=48 << 20),
        name="experts",
    )(tokens, gain.reshape(1, width), w_gate, w_up, w_down)


def on_device(
    x_in,
    routes,
    conv_state,
    ssm_state,
    mamba_gain,
    in_x,
    in_z,
    conv_w,
    conv_b,
    xproj_dt,
    xproj_bc,
    dt_proj,
    dt_bias,
    a_rate,
    d_skip,
    out_proj,
    moe_gain,
    router,
    w_gate,
    w_up,
    w_down,
):
    tok_count, half_width = x_in.shape
    requests = conv_state.shape[0]
    channels = in_x.shape[1]
    owners = lax.axis_size("expert")
    expert = lax.axis_index("expert")
    core = lax.axis_index("cuts")
    half = owners // 2
    perm = ring_perm(owners)
    ahead = ring_ahead(expert, core, owners)
    behind = ring_ahead(expert, 1 - core, owners)
    places = jnp.stack(ahead + [core]).astype(jnp.int32)
    out_other = over_cuts(out_proj)
    full_x = gather_tokens(x_in, owners, core, ahead, behind, perm)
    normed = rms_norm(full_x, mamba_gain)
    u_pre = jnp.dot(normed, in_x, preferred_element_type=F32)
    seq = jnp.concatenate([conv_state, u_pre.reshape(requests, DRAFT, channels)], axis=1)
    conv = jnp.zeros((requests, DRAFT, channels), F32) + conv_b
    for tap in range(conv_w.shape[0]):
        conv = conv + conv_w[tap] * seq[:, tap : tap + DRAFT]
    u_act = jax.nn.silu(conv).astype(BF16)
    flat_u = u_act.reshape(requests * DRAFT, channels)
    rank = xproj_dt.shape[1]
    carried = xproj_bc.shape[1]
    notes = find_slots(routes)
    slot = notes[:, 0]
    notes = jnp.where(core == 0, notes, 0.0)
    tokens = flat_u.shape[0]
    notes = lax.dynamic_update_slice(
        jnp.zeros((tokens, notes.shape[1]), F32), notes, (expert * tok_count, 0)
    )
    part = jnp.concatenate(
        [
            jnp.dot(flat_u, xproj_dt, preferred_element_type=F32),
            jnp.dot(flat_u, xproj_bc, preferred_element_type=F32),
            notes,
        ],
        axis=1,
    )
    holders = owners // EXPERTS
    own = expert // holders
    partner = expert + holders * (1 - 2 * own)
    x_partner = lax.dynamic_slice(
        full_x, (partner * tok_count, core * half_width), (tok_count, half_width)
    )
    part, x_partner = lax.optimization_barrier((part, x_partner))
    total, (z_gate,) = sum_all(
        part,
        owners,
        expert,
        core,
        [lambda: jnp.dot(normed, in_z, preferred_element_type=F32)],
    )
    gated, new_state = scan(
        total, dt_proj, dt_bias, flat_u, z_gate, ssm_state, a_rate, d_skip
    )
    gated = gated.astype(BF16)
    notes = total[:, rank + carried :]
    ids = (jnp.arange(tokens) // tok_count * tok_count).astype(jnp.int32)[:, None] + notes[
        :, :1
    ].astype(jnp.int32)
    near, far, own_term, other = project_blocks(
        ids,
        gated,
        over_cuts(gated),
        out_proj,
        out_other,
        tok_count,
        half,
        places,
    )
    row = jnp.arange(tok_count, dtype=jnp.int32)
    rows_here = (slot_keys(expert, row, holders, tok_count)[:, None] == ids[:, 0][None, :]).astype(
        BF16
    )
    x_rows = jnp.dot(
        lax.dynamic_slice_in_dim(rows_here, expert * tok_count, tok_count, 1),
        x_in,
        preferred_element_type=F32,
    ) + jnp.dot(
        lax.dynamic_slice_in_dim(rows_here, partner * tok_count, tok_count, 1),
        x_partner,
        preferred_element_type=F32,
    )
    route_rows = jnp.dot(rows_here, notes[:, 1:], preferred_element_type=F32).astype(jnp.int32)
    mixed_half = scatter_sum(near, far, own_term, other, tok_count, owners, perm)
    stream_half = (x_rows + mixed_half).astype(BF16)

    def exchange(value, flip):
        return over_expert(value, flip, owners)

    pieces = [stream_half] + [exchange(stream_half, flip) for flip in range(1, holders)]
    tokens_half = jnp.concatenate(pieces, axis=0)
    routed = halves(tokens_half, over_cuts(tokens_half), core)
    partial_out = run_experts(routed, moe_gain, w_gate, w_up, w_down)
    count = partial_out.shape[0]
    mine = lax.dynamic_slice(partial_out, (0, core * half_width), (count, half_width))
    theirs = lax.dynamic_slice(partial_out, (0, (1 - core) * half_width), (count, half_width))
    summed = mine + over_cuts(theirs.astype(BF16)).astype(F32)
    summed = summed.reshape(holders, 2 * CAP, half_width)
    result = summed[0]
    for flip in range(1, holders):
        result = result + exchange(summed[flip].astype(BF16), flip).astype(F32)
    expert_out = result.astype(BF16).astype(F32)

    logits = jnp.dot(
        rms_norm(routed[:tok_count], moe_gain), router, preferred_element_type=F32
    )
    all_labels = jnp.arange(router.shape[1], dtype=jnp.int32)
    which = (route_rows[:, :, None] == all_labels).astype(F32)
    chosen = jnp.sum(logits[:, None, :] * which, axis=-1)
    weight0 = jax.nn.sigmoid(chosen[:, 0] - chosen[:, 1])
    weights = jnp.stack([weight0, 1.0 - weight0], axis=1)
    weight = jnp.sum(jnp.where(route_rows < EXPERTS, weights, 0.0), axis=1)
    done = (stream_half.astype(F32) + weight[:, None] * expert_out).astype(BF16)
    back = exchange(done[CAP:], holders)
    table = jnp.concatenate([done[:CAP], back], axis=0)
    wanted = slot.astype(jnp.int32)
    wanted = jnp.where(own == 0, wanted, (wanted + CAP) % (EXPERTS * CAP))
    pick = (wanted[:, None] == row[None, :]).astype(BF16)
    out = jnp.dot(pick, table, preferred_element_type=F32).astype(BF16)
    return (out, new_state)


def solution(mesh):
    return jax.shard_map(
        on_device,
        mesh=mesh,
        in_specs=(
            P(("group", "expert"), "cuts"),
            P(("group", "expert"), None),
            P("group", None, ("expert", "cuts")),
            P("group", None, ("expert", "cuts")),
            P(),
            P(None, ("expert", "cuts")),
            P(None, ("expert", "cuts")),
            P(None, ("expert", "cuts")),
            P(("expert", "cuts")),
            P(("expert", "cuts"), None),
            P(("expert", "cuts"), None),
            P(None, ("expert", "cuts")),
            P(("expert", "cuts")),
            P(None, ("expert", "cuts")),
            P(("expert", "cuts")),
            P(("expert", "cuts"), None),
            P(),
            P(),
            P(None, ("expert", "cuts")),
            P(None, ("expert", "cuts")),
            P(("expert", "cuts"), None),
        ),
        out_specs=(P(("group", "expert"), "cuts"), P("group", None, ("expert", "cuts"))),
        check_vma=False,
    )
```

```python
import functools

import jax
import jax.numpy as jnp
from jax import lax
from jax.experimental import pallas as pl
from jax.experimental.pallas import tpu as pltpu
from jax.sharding import PartitionSpec as P

EXPERTS = 2
DRAFT = 8
CAP = 16
F32 = jnp.float32
BF16 = jnp.bfloat16
VMEM_LIMIT = 28 << 20


def ring_place(index, owners):
    if owners == 8:
        low = index % 2
        return index // 2 * (1 - 2 * low) + 7 * low
    return index


def ring_index(place, owners):
    if owners == 8:
        low = place // 4
        return 2 * place * (1 - 2 * low) + 15 * low
    return place


def ring_perm(owners):
    pairs = []
    for index in range(owners):
        for core in range(2):
            to = ring_index((ring_place(index, owners) + 1 - 2 * core) % owners, owners)
            pairs.append((2 * index + core, 2 * to + core))
    return pairs


def ring_ahead(expert, core, owners):
    place = ring_place(expert, owners)
    return [
        ring_index(lax.rem(place + (1 - 2 * core) * d + owners, owners), owners)
        for d in range(owners // 2 + 1)
    ]


def over_cuts(value):
    return lax.ppermute(value, "cuts", [(0, 1), (1, 0)])


def over_expert(value, flip, owners):
    return lax.ppermute(value, "expert", [(i, i ^ flip) for i in range(owners)])


def rms_norm(values, gain):
    values = values.astype(F32)
    scale = lax.rsqrt(jnp.mean(values * values, axis=-1, keepdims=True) + 1e-05)
    return (values * scale * gain).astype(BF16)


def halves(first, second, core):
    return jnp.concatenate(
        [jnp.where(core == 0, first, second), jnp.where(core == 0, second, first)], axis=-1
    )


def gather_tokens(x_in, owners, core, ahead, behind, perm):
    half = owners // 2
    rows, width = x_in.shape

    def send(value):
        return lax.ppermute(value, ("expert", "cuts"), perm)

    other = over_cuts(x_in)
    part_a, part_b = [x_in], [other]
    for step in range(1, half + 1):
        part_a.append(send(part_a[-1]))
        if step < half:
            part_b.append(send(part_b[-1]))
    part_b, near = lax.optimization_barrier((part_b, part_a[:half]))
    part_a = [*near, part_a[half]]
    mine = [halves(part_a[d], part_b[d], core) for d in range(half)]
    stack = jnp.concatenate(mine[1:], axis=0)
    theirs = over_cuts(stack).reshape(half - 1, rows, 2 * width)
    far = halves(part_a[half], over_cuts(part_a[half]), core)
    out = jnp.zeros((owners * rows, 2 * width), x_in.dtype)

    def put(buffer, block, index):
        return lax.dynamic_update_slice(buffer, block, (index * rows, 0))

    out = put(out, mine[0], ahead[0])
    for d in range(1, half):
        out = put(out, mine[d], behind[d])
        out = put(out, theirs[d - 1], ahead[d])
    return put(out, far, ahead[half])


def sum_all(part, owners, expert, core, under):
    done = []

    def beside(value):
        if not under:
            return value
        value, extra = lax.optimization_barrier((value, under.pop(0)()))
        done.append(extra)
        return value

    def split(value, bit):
        size = value.shape[0] // 2
        return (
            lax.dynamic_slice_in_dim(value, bit * size, size, 0),
            lax.dynamic_slice_in_dim(value, (1 - bit) * size, size, 0),
        )

    def join(mine, theirs, bit):
        size = mine.shape[0]
        out = jnp.zeros((2 * size,) + mine.shape[1:], mine.dtype)
        out = lax.dynamic_update_slice_in_dim(out, mine, bit * size, 0)
        return lax.dynamic_update_slice_in_dim(out, theirs, (1 - bit) * size, 0)

    keep, give = split(part, core)
    keep = keep + over_cuts(give.astype(BF16)).astype(F32)
    low = expert % 2
    keep, give = split(keep, low)
    keep = keep + beside(over_expert(give.astype(BF16), 1, owners)).astype(F32)
    flip = 2
    while flip < owners:
        keep = keep + beside(over_expert(keep.astype(BF16), flip, owners)).astype(F32)
        flip *= 2
    keep = keep.astype(BF16)
    keep = join(keep, beside(over_expert(keep, 1, owners)), low)
    return (keep, over_cuts(keep)), done


def scan_kernel(
    place_ref,
    mine,
    theirs,
    dt_proj,
    dt_bias,
    u_ref,
    z_hbm,
    state_hbm,
    a_rate,
    d_skip,
    gated,
    new_state,
    notes,
    total,
    z_ref,
    state_ref,
    b_all,
    c_all,
    dt_all,
    sems,
):
    fetches = [
        pltpu.make_async_copy(state_hbm, state_ref, sems.at[0]),
        pltpu.make_async_copy(z_hbm, z_ref, sems.at[1]),
    ]
    for fetch in fetches:
        fetch.start()
    tokens, channels = u_ref.shape
    states = a_rate.shape[0]
    rank = dt_proj.shape[0]
    count = tokens // 2
    core = place_ref[place_ref.shape[0] - 1]
    total[pl.ds(pl.multiple_of(core * count, count), count), :] = mine[...]
    total[pl.ds(pl.multiple_of((1 - core) * count, count), count), :] = theirs[...]
    raw = jnp.dot(total[:, :rank], dt_proj[...], preferred_element_type=F32) + dt_bias[...]
    dt_all[...] = jnp.maximum(raw, 0.0) + jnp.log1p(jnp.exp(-jnp.abs(raw)))
    notes[...] = total[:, rank + 2 * states :].astype(F32)
    ones = jnp.ones((states, channels), BF16)
    diagonal = lax.broadcasted_iota(jnp.int32, (tokens, states, states), 1) == lax.broadcasted_iota(
        jnp.int32, (tokens, states, states), 2
    )
    maps = total[:, rank : rank + 2 * states].astype(F32)
    for start, dest in ((0, b_all), (states, c_all)):
        spread = jnp.broadcast_to(
            maps[:, None, start : start + states], (tokens, states, states)
        )
        spread = jnp.where(diagonal, spread, 0.0).reshape(tokens * states, states).astype(BF16)
        dest[...] = jnp.dot(spread, ones, preferred_element_type=F32)
    for fetch in fetches:
        fetch.wait()
    rate = -a_rate[...]
    skip = d_skip[...]

    def request(r, carry):
        at = pl.ds(pl.multiple_of(r * DRAFT, DRAFT), DRAFT)
        dt = dt_all[at, :]
        u = u_ref[at, :].astype(F32)
        du = dt * u
        state = state_ref[r]
        out = []
        for p in range(DRAFT):
            spot = pl.ds(pl.multiple_of((r * DRAFT + p) * states, states), states)
            state = jnp.exp(dt[p : p + 1] * rate) * state + du[p : p + 1] * b_all[spot, :]
            out.append(jnp.sum(c_all[spot, :] * state, axis=0, keepdims=True))
        new_state[r] = state
        z = z_ref[at, :]
        y = jnp.concatenate(out, axis=0) + skip * u
        gated[at, :] = y * (z * jax.nn.sigmoid(z))
        return carry

    lax.fori_loop(0, tokens // DRAFT, request, 0, unroll=2)


def scan(places, total, dt_proj, dt_bias, u, z, ssm_state, a_rate, d_skip):
    tokens, channels = u.shape
    states = a_rate.shape[0]
    columns = total[0].shape[1]
    extra = columns - dt_proj.shape[0] - 2 * states
    vmem = pl.BlockSpec(memory_space=pltpu.VMEM)
    return pl.pallas_call(
        scan_kernel,
        out_shape=(
            jax.ShapeDtypeStruct((tokens, channels), F32),
            jax.ShapeDtypeStruct(ssm_state.shape, F32),
            jax.ShapeDtypeStruct((tokens, extra), F32),
        ),
        in_specs=[pl.BlockSpec(memory_space=pltpu.SMEM)]
        + [vmem] * 5
        + [pl.BlockSpec(memory_space=pltpu.HBM)] * 2
        + [vmem] * 2,
        out_specs=[vmem] * 3,
        scratch_shapes=[
            pltpu.VMEM((tokens, columns), BF16),
            pltpu.VMEM((tokens, channels), F32),
            pltpu.VMEM(ssm_state.shape, F32),
            pltpu.VMEM((tokens * states, channels), F32),
            pltpu.VMEM((tokens * states, channels), F32),
            pltpu.VMEM((tokens, channels), F32),
            pltpu.SemaphoreType.DMA((2,)),
        ],
        compiler_params=pltpu.CompilerParams(vmem_limit_bytes=VMEM_LIMIT),
        name="scan",
    )(
        places,
        *total,
        dt_proj,
        dt_bias.reshape(1, -1),
        u,
        z,
        ssm_state,
        a_rate,
        d_skip.reshape(1, -1),
    )


def project_kernel(
    half, rows, width, place_ref, id_ref, g_ref, h_ref, wg_ref, wh_ref, near_ref, far_ref, own_ref, other_ref
):
    core = place_ref[half + 1]
    holders = 2 * half // EXPERTS
    ids = id_ref[...]
    column = lax.broadcasted_iota(jnp.int32, (1, (half + 1) * rows), 1)
    target = jnp.zeros_like(column)
    for d in range(half + 1):
        target = jnp.where(column // rows == d, place_ref[d], target)
    picked = (ids == slot_keys(target, column % rows, holders, rows)).astype(F32).astype(BF16)
    here = pl.multiple_of(core * width, 128)
    there = pl.multiple_of((1 - core) * width, 128)
    first = (((0,), (0,)), ((), ()))
    lhs_g = lax.dot_general(picked, g_ref[...], first, preferred_element_type=F32).astype(BF16)
    lhs_h = lax.dot_general(picked, h_ref[...], first, preferred_element_type=F32).astype(BF16)
    tile = 512
    for start in range(0, width, tile):
        at = pl.ds(here + start, tile)
        term = jnp.dot(lhs_g, wg_ref[:, at], preferred_element_type=F32) + jnp.dot(
            lhs_h, wh_ref[:, at], preferred_element_type=F32
        )
        own_ref[:, start : start + tile] = term[:rows]
        near_ref[:, start : start + tile] = term[rows : half * rows]
        far_ref[:, start : start + tile] = term[half * rows :].astype(BF16)
        at = pl.ds(there + start, tile)
        term = jnp.dot(
            lhs_g[rows : half * rows], wg_ref[:, at], preferred_element_type=F32
        ) + jnp.dot(lhs_h[rows : half * rows], wh_ref[:, at], preferred_element_type=F32)
        other_ref[:, start : start + tile] = term


def slots_kernel(routes_ref, out_ref):
    routes = routes_ref[...]
    count = routes.shape[0]
    named = [
        jnp.any(routes == label, axis=1, keepdims=True).astype(F32) for label in range(EXPERTS)
    ]
    idle = 1.0 - named[0] - named[1]
    lane = lax.broadcasted_iota(jnp.int32, (count, 128), 1)
    kinds = jnp.where(lane == 0, named[0], jnp.where(lane == 1, named[1], idle)).astype(BF16)
    earlier = (
        lax.broadcasted_iota(jnp.int32, (count, count), 0)
        > lax.broadcasted_iota(jnp.int32, (count, count), 1)
    )
    ranks = jnp.dot(
        earlier.astype(F32).astype(BF16), kinds, preferred_element_type=F32
    )
    first = jnp.sum(named[0], axis=0, keepdims=True)
    second = jnp.sum(named[1], axis=0, keepdims=True)
    spare = jnp.where(second < CAP, CAP + second, first)
    slot = (
        named[0] * ranks[:, 0:1]
        + named[1] * (CAP + ranks[:, 1:2])
        + idle * (spare + ranks[:, 2:3])
    )
    both = routes.astype(F32)
    out_ref[...] = jnp.concatenate([slot, both], axis=1)


def find_slots(routes):
    vmem = pl.BlockSpec(memory_space=pltpu.VMEM)
    return pl.pallas_call(
        slots_kernel,
        out_shape=jax.ShapeDtypeStruct((routes.shape[0], 1 + routes.shape[1]), F32),
        in_specs=[vmem],
        out_specs=vmem,
        compiler_params=pltpu.CompilerParams(vmem_limit_bytes=1 << 20),
        name="slots",
    )(routes)


def slot_keys(target, row, holders, rows):
    expert = target // holders
    block = jnp.where(row < CAP, target, target + holders * (1 - 2 * expert))
    return block * rows + expert * CAP + row % CAP


def project_blocks(ids, gated, gated_other, out_proj, out_other, rows, half, places):
    width = out_proj.shape[1] // 2
    vmem = pl.BlockSpec(memory_space=pltpu.VMEM)
    return pl.pallas_call(
        functools.partial(project_kernel, half, rows, width),
        out_shape=(
            jax.ShapeDtypeStruct(((half - 1) * rows, width), F32),
            jax.ShapeDtypeStruct((rows, width), BF16),
            jax.ShapeDtypeStruct((rows, width), F32),
            jax.ShapeDtypeStruct(((half - 1) * rows, width), F32),
        ),
        in_specs=[pl.BlockSpec(memory_space=pltpu.SMEM)] + [vmem] * 5,
        out_specs=[vmem] * 4,
        compiler_params=pltpu.CompilerParams(vmem_limit_bytes=VMEM_LIMIT),
        name="project",
    )(places, ids, gated, gated_other, out_proj, out_other)


def scatter_sum(near, far, own, other, rows, owners, perm):
    half = owners // 2

    def send(value):
        return lax.ppermute(value.astype(BF16), ("expert", "cuts"), perm)

    acc_a = send(far)
    acc_b = None
    for d in range(half - 1, 0, -1):
        at = slice((d - 1) * rows, d * rows)
        acc_a = send(acc_a.astype(F32) + near[at])
        acc_b = send(other[at] if acc_b is None else acc_b.astype(F32) + other[at])
    return own + acc_a.astype(F32) + over_cuts(acc_b).astype(F32)


def experts_kernel(tiles, pieces, place_ref, *refs):
    own, refs = refs[:pieces], refs[pieces:]
    other, refs = refs[:pieces], refs[pieces:]
    gain_ref, wg_hbm, wu_hbm, wd_hbm, out_ref, x_ref, wg, wu, wd, sems = refs
    tile = wg.shape[2]
    copies = []
    for i in range(tiles):
        at = pl.ds(i * tile, tile)
        copies.append(
            (
                pltpu.make_async_copy(wg_hbm.at[:, at], wg.at[i], sems.at[0, i]),
                pltpu.make_async_copy(wu_hbm.at[:, at], wu.at[i], sems.at[1, i]),
                pltpu.make_async_copy(wd_hbm.at[at, :], wd.at[i], sems.at[2, i]),
            )
        )
    for group in copies:
        group[0].start()
        group[1].start()
    for group in copies:
        group[2].start()
    rows, width = own[0].shape
    core = place_ref[place_ref.shape[0] - 1]
    here = pl.ds(pl.multiple_of(core * width, 128), width)
    there = pl.ds(pl.multiple_of((1 - core) * width, 128), width)
    for i in range(pieces):
        x_ref[i * rows : (i + 1) * rows, here] = own[i][...]
        x_ref[i * rows : (i + 1) * rows, there] = other[i][...]
    values = x_ref[...].astype(F32)
    scale = lax.rsqrt(jnp.mean(values * values, axis=-1, keepdims=True) + 1e-05)
    x = (values * scale * gain_ref[...]).astype(BF16)
    acts = []
    for i in range(tiles):
        copies[i][0].wait()
        gate = jnp.dot(x, wg[i], preferred_element_type=F32)
        copies[i][1].wait()
        upval = jnp.dot(x, wu[i], preferred_element_type=F32)
        acts.append((gate * jax.nn.sigmoid(gate) * upval).astype(BF16))
    for i in range(tiles):
        copies[i][2].wait()
        term = jnp.dot(acts[i], wd[i], preferred_element_type=F32)
        if i == 0:
            out_ref[...] = term
        else:
            out_ref[...] += term


def run_experts(places, own, other, gain, w_gate, w_up, w_down):
    pieces = len(own)
    count, width = pieces * own[0].shape[0], 2 * own[0].shape[1]
    hidden = w_gate.shape[1]
    tile = 256
    tiles = hidden // tile
    vmem = pl.BlockSpec(memory_space=pltpu.VMEM)
    hbm = pl.BlockSpec(memory_space=pltpu.HBM)
    return pl.pallas_call(
        functools.partial(experts_kernel, tiles, pieces),
        out_shape=jax.ShapeDtypeStruct((count, width), F32),
        in_specs=[pl.BlockSpec(memory_space=pltpu.SMEM)] + [vmem] * (2 * pieces + 1) + [hbm] * 3,
        out_specs=vmem,
        scratch_shapes=[
            pltpu.VMEM((count, width), BF16),
            pltpu.VMEM((tiles, width, tile), BF16),
            pltpu.VMEM((tiles, width, tile), BF16),
            pltpu.VMEM((tiles, tile, width), BF16),
            pltpu.SemaphoreType.DMA((3, tiles)),
        ],
        compiler_params=pltpu.CompilerParams(vmem_limit_bytes=48 << 20),
        name="experts",
    )(places, *own, *other, gain.reshape(1, width), w_gate, w_up, w_down)


def on_device(
    x_in,
    routes,
    conv_state,
    ssm_state,
    mamba_gain,
    in_x,
    in_z,
    conv_w,
    conv_b,
    xproj_dt,
    xproj_bc,
    dt_proj,
    dt_bias,
    a_rate,
    d_skip,
    out_proj,
    moe_gain,
    router,
    w_gate,
    w_up,
    w_down,
):
    tok_count, half_width = x_in.shape
    requests = conv_state.shape[0]
    channels = in_x.shape[1]
    owners = lax.axis_size("expert")
    expert = lax.axis_index("expert")
    core = lax.axis_index("cuts")
    half = owners // 2
    perm = ring_perm(owners)
    ahead = ring_ahead(expert, core, owners)
    behind = ring_ahead(expert, 1 - core, owners)
    places = jnp.stack(ahead + [core]).astype(jnp.int32)
    out_other = over_cuts(out_proj)
    full_x = gather_tokens(x_in, owners, core, ahead, behind, perm)
    normed = rms_norm(full_x, mamba_gain)
    u_pre = jnp.dot(normed, in_x, preferred_element_type=F32)
    seq = jnp.concatenate([conv_state, u_pre.reshape(requests, DRAFT, channels)], axis=1)
    conv = jnp.zeros((requests, DRAFT, channels), F32) + conv_b
    for tap in range(conv_w.shape[0]):
        conv = conv + conv_w[tap] * seq[:, tap : tap + DRAFT]
    u_act = jax.nn.silu(conv).astype(BF16)
    flat_u = u_act.reshape(requests * DRAFT, channels)
    rank = xproj_dt.shape[1]
    notes = find_slots(routes)
    slot = notes[:, 0]
    notes = jnp.where(core == 0, notes, 0.0)
    tokens = flat_u.shape[0]
    notes = lax.dynamic_update_slice(
        jnp.zeros((tokens, notes.shape[1]), F32), notes, (expert * tok_count, 0)
    )
    part = jnp.concatenate(
        [
            jnp.dot(flat_u, xproj_dt, preferred_element_type=F32),
            jnp.dot(flat_u, xproj_bc, preferred_element_type=F32),
            notes,
        ],
        axis=1,
    )
    holders = owners // EXPERTS
    own = expert // holders
    partner = expert + holders * (1 - 2 * own)
    x_partner = lax.dynamic_slice(
        full_x, (partner * tok_count, core * half_width), (tok_count, half_width)
    )
    part, x_partner = lax.optimization_barrier((part, x_partner))
    total, (z_gate,) = sum_all(
        part,
        owners,
        expert,
        core,
        [lambda: jnp.dot(normed, in_z, preferred_element_type=F32)],
    )
    gated, new_state, notes = scan(
        places, total, dt_proj, dt_bias, flat_u, z_gate, ssm_state, a_rate, d_skip
    )
    gated = gated.astype(BF16)
    ids = (jnp.arange(tokens) // tok_count * tok_count).astype(jnp.int32)[:, None] + notes[
        :, :1
    ].astype(jnp.int32)
    near, far, own_term, other = project_blocks(
        ids,
        gated,
        over_cuts(gated),
        out_proj,
        out_other,
        tok_count,
        half,
        places,
    )
    row = jnp.arange(tok_count, dtype=jnp.int32)
    rows_here = (slot_keys(expert, row, holders, tok_count)[:, None] == ids[:, 0][None, :]).astype(
        BF16
    )
    x_rows = jnp.dot(
        lax.dynamic_slice_in_dim(rows_here, expert * tok_count, tok_count, 1),
        x_in,
        preferred_element_type=F32,
    ) + jnp.dot(
        lax.dynamic_slice_in_dim(rows_here, partner * tok_count, tok_count, 1),
        x_partner,
        preferred_element_type=F32,
    )
    route_rows = jnp.dot(rows_here, notes[:, 1:].astype(BF16), preferred_element_type=F32).astype(jnp.int32)
    mixed_half = scatter_sum(near, far, own_term, other, tok_count, owners, perm)
    stream_half = (x_rows + mixed_half).astype(BF16)

    def exchange(value, flip):
        return over_expert(value, flip, owners)

    pieces = [stream_half] + [exchange(stream_half, flip) for flip in range(1, holders)]
    others = [over_cuts(piece) for piece in pieces]
    partial_out = run_experts(places, pieces, others, moe_gain, w_gate, w_up, w_down)
    count = partial_out.shape[0]
    mine = lax.dynamic_slice(partial_out, (0, core * half_width), (count, half_width))
    theirs = lax.dynamic_slice(partial_out, (0, (1 - core) * half_width), (count, half_width))
    summed = mine + over_cuts(theirs.astype(BF16)).astype(F32)
    summed = summed.reshape(holders, 2 * CAP, half_width)
    result = summed[0]
    for flip in range(1, holders):
        result = result + exchange(summed[flip].astype(BF16), flip).astype(F32)
    expert_out = result.astype(BF16).astype(F32)

    logits = jnp.dot(
        rms_norm(halves(stream_half, others[0], core), moe_gain), router, preferred_element_type=F32
    )
    all_labels = jnp.arange(router.shape[1], dtype=jnp.int32)
    which = (route_rows[:, :, None] == all_labels).astype(F32)
    chosen = jnp.sum(logits[:, None, :] * which, axis=-1)
    weight0 = jax.nn.sigmoid(chosen[:, 0] - chosen[:, 1])
    weights = jnp.stack([weight0, 1.0 - weight0], axis=1)
    weight = jnp.sum(jnp.where(route_rows < EXPERTS, weights, 0.0), axis=1)
    done = (stream_half.astype(F32) + weight[:, None] * expert_out).astype(BF16)
    back = exchange(done[CAP:], holders)
    table = jnp.concatenate([done[:CAP], back], axis=0)
    wanted = slot.astype(jnp.int32)
    wanted = jnp.where(own == 0, wanted, (wanted + CAP) % (EXPERTS * CAP))
    pick = (wanted[:, None] == row[None, :]).astype(BF16)
    out = jnp.dot(pick, table, preferred_element_type=F32).astype(BF16)
    return (out, new_state)


def solution(mesh):
    return jax.shard_map(
        on_device,
        mesh=mesh,
        in_specs=(
            P(("group", "expert"), "cuts"),
            P(("group", "expert"), None),
            P("group", None, ("expert", "cuts")),
            P("group", None, ("expert", "cuts")),
            P(),
            P(None, ("expert", "cuts")),
            P(None, ("expert", "cuts")),
            P(None, ("expert", "cuts")),
            P(("expert", "cuts")),
            P(("expert", "cuts"), None),
            P(("expert", "cuts"), None),
            P(None, ("expert", "cuts")),
            P(("expert", "cuts")),
            P(None, ("expert", "cuts")),
            P(("expert", "cuts")),
            P(("expert", "cuts"), None),
            P(),
            P(),
            P(None, ("expert", "cuts")),
            P(None, ("expert", "cuts")),
            P(("expert", "cuts"), None),
        ),
        out_specs=(P(("group", "expert"), "cuts"), P("group", None, ("expert", "cuts"))),
        check_vma=False,
    )
```

```python
import functools

import jax
import jax.numpy as jnp
from jax import lax
from jax.experimental import pallas as pl
from jax.experimental.pallas import tpu as pltpu
from jax.sharding import PartitionSpec as P

EXPERTS = 2
DRAFT = 8
CAP = 16
F32 = jnp.float32
BF16 = jnp.bfloat16
VMEM_LIMIT = 28 << 20


def ring_place(index, owners):
    if owners == 8:
        low = index % 2
        return index // 2 * (1 - 2 * low) + 7 * low
    return index


def ring_index(place, owners):
    if owners == 8:
        low = place // 4
        return 2 * place * (1 - 2 * low) + 15 * low
    return place


def ring_perm(owners):
    pairs = []
    for index in range(owners):
        for core in range(2):
            to = ring_index((ring_place(index, owners) + 1 - 2 * core) % owners, owners)
            pairs.append((2 * index + core, 2 * to + core))
    return pairs


def ring_ahead(expert, core, owners):
    place = ring_place(expert, owners)
    return [
        ring_index(lax.rem(place + (1 - 2 * core) * d + owners, owners), owners)
        for d in range(owners // 2 + 1)
    ]


def over_cuts(value):
    return lax.ppermute(value, "cuts", [(0, 1), (1, 0)])


def over_expert(value, flip, owners):
    return lax.ppermute(value, "expert", [(i, i ^ flip) for i in range(owners)])


def rms_norm(values, gain):
    values = values.astype(F32)
    scale = lax.rsqrt(jnp.mean(values * values, axis=-1, keepdims=True) + 1e-05)
    return (values * scale * gain).astype(BF16)


def halves(first, second, core):
    return jnp.concatenate(
        [jnp.where(core == 0, first, second), jnp.where(core == 0, second, first)], axis=-1
    )


def gather_tokens(x_in, owners, core, ahead, behind, perm):
    half = owners // 2
    rows, width = x_in.shape

    def send(value):
        return lax.ppermute(value, ("expert", "cuts"), perm)

    other = over_cuts(x_in)
    part_a, part_b = [x_in], [other]
    for step in range(1, half + 1):
        part_a.append(send(part_a[-1]))
        if step < half:
            part_b.append(send(part_b[-1]))
    part_b, near = lax.optimization_barrier((part_b, part_a[:half]))
    part_a = [*near, part_a[half]]
    mine = [halves(part_a[d], part_b[d], core) for d in range(half)]
    stack = jnp.concatenate(mine[1:], axis=0)
    theirs = over_cuts(stack).reshape(half - 1, rows, 2 * width)
    far = halves(part_a[half], over_cuts(part_a[half]), core)
    out = jnp.zeros((owners * rows, 2 * width), x_in.dtype)

    def put(buffer, block, index):
        return lax.dynamic_update_slice(buffer, block, (index * rows, 0))

    out = put(out, mine[0], ahead[0])
    for d in range(1, half):
        out = put(out, mine[d], behind[d])
        out = put(out, theirs[d - 1], ahead[d])
    return put(out, far, ahead[half])


def sum_all(part, owners, expert, core, under):
    done = []

    def beside(value):
        if not under:
            return value
        value, extra = lax.optimization_barrier((value, under.pop(0)()))
        done.append(extra)
        return value

    def split(value, bit):
        size = value.shape[0] // 2
        return (
            lax.dynamic_slice_in_dim(value, bit * size, size, 0),
            lax.dynamic_slice_in_dim(value, (1 - bit) * size, size, 0),
        )

    def join(mine, theirs, bit):
        size = mine.shape[0]
        out = jnp.zeros((2 * size,) + mine.shape[1:], mine.dtype)
        out = lax.dynamic_update_slice_in_dim(out, mine, bit * size, 0)
        return lax.dynamic_update_slice_in_dim(out, theirs, (1 - bit) * size, 0)

    keep, give = split(part, core)
    keep = keep + over_cuts(give.astype(BF16)).astype(F32)
    low = expert % 2
    keep, give = split(keep, low)
    keep = keep + beside(over_expert(give.astype(BF16), 1, owners)).astype(F32)
    flip = 2
    while flip < owners:
        keep = keep + beside(over_expert(keep.astype(BF16), flip, owners)).astype(F32)
        flip *= 2
    keep = keep.astype(BF16)
    keep = join(keep, beside(over_expert(keep, 1, owners)), low)
    return (keep, over_cuts(keep)), done


def scan_kernel(
    place_ref,
    mine,
    theirs,
    dt_proj,
    dt_bias,
    u_ref,
    z_hbm,
    state_hbm,
    a_rate,
    d_skip,
    gated,
    new_state,
    notes,
    total,
    z_ref,
    state_ref,
    b_all,
    c_all,
    dt_all,
    sems,
):
    fetches = [
        pltpu.make_async_copy(state_hbm, state_ref, sems.at[0]),
        pltpu.make_async_copy(z_hbm, z_ref, sems.at[1]),
    ]
    for fetch in fetches:
        fetch.start()
    tokens, channels = u_ref.shape
    states = a_rate.shape[0]
    rank = dt_proj.shape[0]
    count = tokens // 2
    core = place_ref[place_ref.shape[0] - 1]
    total[pl.ds(pl.multiple_of(core * count, count), count), :] = mine[...]
    total[pl.ds(pl.multiple_of((1 - core) * count, count), count), :] = theirs[...]
    raw = jnp.dot(total[:, :rank], dt_proj[...], preferred_element_type=F32) + dt_bias[...]
    dt_all[...] = jnp.maximum(raw, 0.0) + jnp.log1p(jnp.exp(-jnp.abs(raw)))
    notes[...] = total[:, rank + 2 * states :].astype(F32)
    ones = jnp.ones((states, channels), BF16)
    diagonal = lax.broadcasted_iota(jnp.int32, (tokens, states, states), 1) == lax.broadcasted_iota(
        jnp.int32, (tokens, states, states), 2
    )
    maps = total[:, rank : rank + 2 * states].astype(F32)
    for start, dest in ((0, b_all), (states, c_all)):
        spread = jnp.broadcast_to(
            maps[:, None, start : start + states], (tokens, states, states)
        )
        spread = jnp.where(diagonal, spread, 0.0).reshape(tokens * states, states).astype(BF16)
        dest[...] = jnp.dot(spread, ones, preferred_element_type=F32)
    for fetch in fetches:
        fetch.wait()
    rate = -a_rate[...]
    skip = d_skip[...]

    def request(r, carry):
        at = pl.ds(pl.multiple_of(r * DRAFT, DRAFT), DRAFT)
        dt = dt_all[at, :]
        u = u_ref[at, :].astype(F32)
        du = dt * u
        state = state_ref[r]
        out = []
        for p in range(DRAFT):
            spot = pl.ds(pl.multiple_of((r * DRAFT + p) * states, states), states)
            state = jnp.exp(dt[p : p + 1] * rate) * state + du[p : p + 1] * b_all[spot, :]
            out.append(jnp.sum(c_all[spot, :] * state, axis=0, keepdims=True))
        new_state[r] = state
        z = z_ref[at, :]
        y = jnp.concatenate(out, axis=0) + skip * u
        gated[at, :] = y * (z * jax.nn.sigmoid(z))
        return carry

    lax.fori_loop(0, tokens // DRAFT, request, 0, unroll=4)


def scan(places, total, dt_proj, dt_bias, u, z, ssm_state, a_rate, d_skip):
    tokens, channels = u.shape
    states = a_rate.shape[0]
    columns = total[0].shape[1]
    extra = columns - dt_proj.shape[0] - 2 * states
    vmem = pl.BlockSpec(memory_space=pltpu.VMEM)
    return pl.pallas_call(
        scan_kernel,
        out_shape=(
            jax.ShapeDtypeStruct((tokens, channels), F32),
            jax.ShapeDtypeStruct(ssm_state.shape, F32),
            jax.ShapeDtypeStruct((tokens, extra), F32),
        ),
        in_specs=[pl.BlockSpec(memory_space=pltpu.SMEM)]
        + [vmem] * 5
        + [pl.BlockSpec(memory_space=pltpu.HBM)] * 2
        + [vmem] * 2,
        out_specs=[vmem] * 3,
        scratch_shapes=[
            pltpu.VMEM((tokens, columns), BF16),
            pltpu.VMEM((tokens, channels), F32),
            pltpu.VMEM(ssm_state.shape, F32),
            pltpu.VMEM((tokens * states, channels), F32),
            pltpu.VMEM((tokens * states, channels), F32),
            pltpu.VMEM((tokens, channels), F32),
            pltpu.SemaphoreType.DMA((2,)),
        ],
        compiler_params=pltpu.CompilerParams(vmem_limit_bytes=VMEM_LIMIT),
        name="scan",
    )(
        places,
        *total,
        dt_proj,
        dt_bias.reshape(1, -1),
        u,
        z,
        ssm_state,
        a_rate,
        d_skip.reshape(1, -1),
    )


def project_kernel(
    half, rows, width, place_ref, id_ref, g_ref, h_ref, wg_ref, wh_ref, near_ref, far_ref, own_ref, other_ref
):
    core = place_ref[half + 1]
    holders = 2 * half // EXPERTS
    ids = id_ref[...]
    column = lax.broadcasted_iota(jnp.int32, (1, (half + 1) * rows), 1)
    target = jnp.zeros_like(column)
    for d in range(half + 1):
        target = jnp.where(column // rows == d, place_ref[d], target)
    picked = (ids == slot_keys(target, column % rows, holders, rows)).astype(F32).astype(BF16)
    here = pl.multiple_of(core * width, 128)
    there = pl.multiple_of((1 - core) * width, 128)
    first = (((0,), (0,)), ((), ()))
    lhs_g = lax.dot_general(picked, g_ref[...], first, preferred_element_type=F32).astype(BF16)
    lhs_h = lax.dot_general(picked, h_ref[...], first, preferred_element_type=F32).astype(BF16)
    tile = 512
    for start in range(0, width, tile):
        at = pl.ds(here + start, tile)
        term = jnp.dot(lhs_g, wg_ref[:, at], preferred_element_type=F32) + jnp.dot(
            lhs_h, wh_ref[:, at], preferred_element_type=F32
        )
        own_ref[:, start : start + tile] = term[:rows]
        near_ref[:, start : start + tile] = term[rows : half * rows]
        far_ref[:, start : start + tile] = term[half * rows :].astype(BF16)
        at = pl.ds(there + start, tile)
        term = jnp.dot(
            lhs_g[rows : half * rows], wg_ref[:, at], preferred_element_type=F32
        ) + jnp.dot(lhs_h[rows : half * rows], wh_ref[:, at], preferred_element_type=F32)
        other_ref[:, start : start + tile] = term


def slots_kernel(routes_ref, out_ref):
    routes = routes_ref[...]
    count = routes.shape[0]
    named = [
        jnp.any(routes == label, axis=1, keepdims=True).astype(F32) for label in range(EXPERTS)
    ]
    idle = 1.0 - named[0] - named[1]
    lane = lax.broadcasted_iota(jnp.int32, (count, 128), 1)
    kinds = jnp.where(lane == 0, named[0], jnp.where(lane == 1, named[1], idle)).astype(BF16)
    earlier = (
        lax.broadcasted_iota(jnp.int32, (count, count), 0)
        > lax.broadcasted_iota(jnp.int32, (count, count), 1)
    )
    ranks = jnp.dot(
        earlier.astype(F32).astype(BF16), kinds, preferred_element_type=F32
    )
    first = jnp.sum(named[0], axis=0, keepdims=True)
    second = jnp.sum(named[1], axis=0, keepdims=True)
    spare = jnp.where(second < CAP, CAP + second, first)
    slot = (
        named[0] * ranks[:, 0:1]
        + named[1] * (CAP + ranks[:, 1:2])
        + idle * (spare + ranks[:, 2:3])
    )
    both = routes.astype(F32)
    out_ref[...] = jnp.concatenate([slot, both], axis=1)


def find_slots(routes):
    vmem = pl.BlockSpec(memory_space=pltpu.VMEM)
    return pl.pallas_call(
        slots_kernel,
        out_shape=jax.ShapeDtypeStruct((routes.shape[0], 1 + routes.shape[1]), F32),
        in_specs=[vmem],
        out_specs=vmem,
        compiler_params=pltpu.CompilerParams(vmem_limit_bytes=1 << 20),
        name="slots",
    )(routes)


def slot_keys(target, row, holders, rows):
    expert = target // holders
    block = jnp.where(row < CAP, target, target + holders * (1 - 2 * expert))
    return block * rows + expert * CAP + row % CAP


def project_blocks(ids, gated, gated_other, out_proj, out_other, rows, half, places):
    width = out_proj.shape[1] // 2
    vmem = pl.BlockSpec(memory_space=pltpu.VMEM)
    return pl.pallas_call(
        functools.partial(project_kernel, half, rows, width),
        out_shape=(
            jax.ShapeDtypeStruct(((half - 1) * rows, width), F32),
            jax.ShapeDtypeStruct((rows, width), BF16),
            jax.ShapeDtypeStruct((rows, width), F32),
            jax.ShapeDtypeStruct(((half - 1) * rows, width), F32),
        ),
        in_specs=[pl.BlockSpec(memory_space=pltpu.SMEM)] + [vmem] * 5,
        out_specs=[vmem] * 4,
        compiler_params=pltpu.CompilerParams(vmem_limit_bytes=14 << 20),
        name="project",
    )(places, ids, gated, gated_other, out_proj, out_other)


def scatter_sum(near, far, own, other, rows, owners, perm):
    half = owners // 2

    def send(value):
        return lax.ppermute(value.astype(BF16), ("expert", "cuts"), perm)

    acc_a = send(far)
    acc_b = None
    for d in range(half - 1, 0, -1):
        at = slice((d - 1) * rows, d * rows)
        acc_a = send(acc_a.astype(F32) + near[at])
        acc_b = send(other[at] if acc_b is None else acc_b.astype(F32) + other[at])
    return own + acc_a.astype(F32) + over_cuts(acc_b).astype(F32)


def experts_kernel(tiles, pieces, place_ref, *refs):
    own, refs = refs[:pieces], refs[pieces:]
    other, refs = refs[:pieces], refs[pieces:]
    gain_ref, wg_hbm, wu_hbm, wd_hbm, out_ref, x_ref, wg, wu, wd, sems = refs
    depth = wg.shape[0] // tiles
    inner = wd.shape[0] // tiles

    def fetch(kind, src, dst, size):
        parts = [pl.ds(i * size, size) for i in range(tiles)]
        return [
            pltpu.make_async_copy(src.at[at, :], dst.at[at, :], sems.at[kind, i])
            for i, at in enumerate(parts)
        ]

    gates = fetch(0, wg_hbm, wg, depth)
    ups = fetch(1, wu_hbm, wu, depth)
    downs = fetch(2, wd_hbm, wd, inner)
    for i in range(tiles):
        gates[i].start()
        ups[i].start()
    for copy in downs:
        copy.start()
    rows, width = own[0].shape
    core = place_ref[place_ref.shape[0] - 1]
    here = pl.ds(pl.multiple_of(core * width, 128), width)
    there = pl.ds(pl.multiple_of((1 - core) * width, 128), width)
    for i in range(pieces):
        x_ref[i * rows : (i + 1) * rows, here] = own[i][...]
        x_ref[i * rows : (i + 1) * rows, there] = other[i][...]
    values = x_ref[...].astype(F32)
    scale = lax.rsqrt(jnp.mean(values * values, axis=-1, keepdims=True) + 1e-05)
    x_ref[...] = (values * scale * gain_ref[...]).astype(BF16)
    gate = upval = None
    for i in range(tiles):
        at = slice(i * depth, (i + 1) * depth)
        gates[i].wait()
        term = jnp.dot(x_ref[:, at], wg[at, :], preferred_element_type=F32)
        gate = term if gate is None else gate + term
        ups[i].wait()
        term = jnp.dot(x_ref[:, at], wu[at, :], preferred_element_type=F32)
        upval = term if upval is None else upval + term
    act = (gate * jax.nn.sigmoid(gate) * upval).astype(BF16)
    for i in range(tiles):
        at = slice(i * inner, (i + 1) * inner)
        downs[i].wait()
        term = jnp.dot(act[:, at], wd[at, :], preferred_element_type=F32)
        if i == 0:
            out_ref[...] = term
        else:
            out_ref[...] += term


def run_experts(places, own, other, gain, w_gate, w_up, w_down):
    pieces = len(own)
    count, width = pieces * own[0].shape[0], 2 * own[0].shape[1]
    tiles = 4
    vmem = pl.BlockSpec(memory_space=pltpu.VMEM)
    hbm = pl.BlockSpec(memory_space=pltpu.HBM)
    return pl.pallas_call(
        functools.partial(experts_kernel, tiles, pieces),
        out_shape=jax.ShapeDtypeStruct((count, width), F32),
        in_specs=[pl.BlockSpec(memory_space=pltpu.SMEM)] + [vmem] * (2 * pieces + 1) + [hbm] * 3,
        out_specs=vmem,
        scratch_shapes=[
            pltpu.VMEM((count, width), BF16),
            pltpu.VMEM(w_gate.shape, BF16),
            pltpu.VMEM(w_up.shape, BF16),
            pltpu.VMEM(w_down.shape, BF16),
            pltpu.SemaphoreType.DMA((3, tiles)),
        ],
        compiler_params=pltpu.CompilerParams(vmem_limit_bytes=28 << 20),
        name="experts",
    )(
        places,
        *own,
        *other,
        gain.reshape(1, width),
        *(pltpu.with_memory_space_constraint(w, pltpu.HBM) for w in (w_gate, w_up, w_down)),
    )


def on_device(
    x_in,
    routes,
    conv_state,
    ssm_state,
    mamba_gain,
    in_x,
    in_z,
    conv_w,
    conv_b,
    xproj_dt,
    xproj_bc,
    dt_proj,
    dt_bias,
    a_rate,
    d_skip,
    out_proj,
    moe_gain,
    router,
    w_gate,
    w_up,
    w_down,
):
    tok_count, half_width = x_in.shape
    requests = conv_state.shape[0]
    channels = in_x.shape[1]
    owners = lax.axis_size("expert")
    expert = lax.axis_index("expert")
    core = lax.axis_index("cuts")
    half = owners // 2
    perm = ring_perm(owners)
    ahead = ring_ahead(expert, core, owners)
    behind = ring_ahead(expert, 1 - core, owners)
    places = jnp.stack(ahead + [core]).astype(jnp.int32)
    out_other = over_cuts(out_proj)
    full_x = gather_tokens(x_in, owners, core, ahead, behind, perm)
    normed = rms_norm(full_x, mamba_gain)
    u_pre = jnp.dot(normed, in_x, preferred_element_type=F32)
    seq = jnp.concatenate([conv_state, u_pre.reshape(requests, DRAFT, channels)], axis=1)
    conv = jnp.zeros((requests, DRAFT, channels), F32) + conv_b
    for tap in range(conv_w.shape[0]):
        conv = conv + conv_w[tap] * seq[:, tap : tap + DRAFT]
    u_act = jax.nn.silu(conv).astype(BF16)
    flat_u = u_act.reshape(requests * DRAFT, channels)
    rank = xproj_dt.shape[1]
    notes = find_slots(routes)
    slot = notes[:, 0]
    notes = jnp.where(core == 0, notes, 0.0)
    tokens = flat_u.shape[0]
    notes = lax.dynamic_update_slice(
        jnp.zeros((tokens, notes.shape[1]), F32), notes, (expert * tok_count, 0)
    )
    part = jnp.concatenate(
        [
            jnp.dot(flat_u, xproj_dt, preferred_element_type=F32),
            jnp.dot(flat_u, xproj_bc, preferred_element_type=F32),
            notes,
        ],
        axis=1,
    )
    holders = owners // EXPERTS
    own = expert // holders
    partner = expert + holders * (1 - 2 * own)
    x_partner = lax.dynamic_slice(
        full_x, (partner * tok_count, core * half_width), (tok_count, half_width)
    )
    part, x_partner = lax.optimization_barrier((part, x_partner))
    total, (z_gate,) = sum_all(
        part,
        owners,
        expert,
        core,
        [lambda: jnp.dot(normed, in_z, preferred_element_type=F32)],
    )
    gated, new_state, notes = scan(
        places, total, dt_proj, dt_bias, flat_u, z_gate, ssm_state, a_rate, d_skip
    )
    gated = gated.astype(BF16)
    ids = (jnp.arange(tokens) // tok_count * tok_count).astype(jnp.int32)[:, None] + notes[
        :, :1
    ].astype(jnp.int32)
    near, far, own_term, other = project_blocks(
        ids,
        gated,
        over_cuts(gated),
        out_proj,
        out_other,
        tok_count,
        half,
        places,
    )
    row = jnp.arange(tok_count, dtype=jnp.int32)
    rows_here = (slot_keys(expert, row, holders, tok_count)[:, None] == ids[:, 0][None, :]).astype(
        BF16
    )
    x_rows = jnp.dot(
        lax.dynamic_slice_in_dim(rows_here, expert * tok_count, tok_count, 1),
        x_in,
        preferred_element_type=F32,
    ) + jnp.dot(
        lax.dynamic_slice_in_dim(rows_here, partner * tok_count, tok_count, 1),
        x_partner,
        preferred_element_type=F32,
    )
    route_rows = jnp.dot(rows_here, notes[:, 1:].astype(BF16), preferred_element_type=F32).astype(jnp.int32)
    mixed_half = scatter_sum(near, far, own_term, other, tok_count, owners, perm)
    stream_half = (x_rows + mixed_half).astype(BF16)

    def exchange(value, flip):
        return over_expert(value, flip, owners)

    pieces = [stream_half] + [exchange(stream_half, flip) for flip in range(1, holders)]
    others = [over_cuts(piece) for piece in pieces]
    partial_out = run_experts(places, pieces, others, moe_gain, w_gate, w_up, w_down)
    count = partial_out.shape[0]
    mine = lax.dynamic_slice(partial_out, (0, core * half_width), (count, half_width))
    theirs = lax.dynamic_slice(partial_out, (0, (1 - core) * half_width), (count, half_width))
    summed = mine + over_cuts(theirs.astype(BF16)).astype(F32)
    summed = summed.reshape(holders, 2 * CAP, half_width)
    result = summed[0]
    for flip in range(1, holders):
        result = result + exchange(summed[flip].astype(BF16), flip).astype(F32)
    expert_out = result.astype(BF16).astype(F32)

    logits = jnp.dot(
        rms_norm(halves(stream_half, others[0], core), moe_gain), router, preferred_element_type=F32
    )
    all_labels = jnp.arange(router.shape[1], dtype=jnp.int32)
    which = (route_rows[:, :, None] == all_labels).astype(F32)
    chosen = jnp.sum(logits[:, None, :] * which, axis=-1)
    weight0 = jax.nn.sigmoid(chosen[:, 0] - chosen[:, 1])
    weights = jnp.stack([weight0, 1.0 - weight0], axis=1)
    weight = jnp.sum(jnp.where(route_rows < EXPERTS, weights, 0.0), axis=1)
    done = (stream_half.astype(F32) + weight[:, None] * expert_out).astype(BF16)
    back = exchange(done[CAP:], holders)
    table = jnp.concatenate([done[:CAP], back], axis=0)
    wanted = slot.astype(jnp.int32)
    wanted = jnp.where(own == 0, wanted, (wanted + CAP) % (EXPERTS * CAP))
    pick = (wanted[:, None] == row[None, :]).astype(BF16)
    out = jnp.dot(pick, table, preferred_element_type=F32).astype(BF16)
    return (out, new_state)


def solution(mesh):
    return jax.shard_map(
        on_device,
        mesh=mesh,
        in_specs=(
            P(("group", "expert"), "cuts"),
            P(("group", "expert"), None),
            P("group", None, ("expert", "cuts")),
            P("group", None, ("expert", "cuts")),
            P(),
            P(None, ("expert", "cuts")),
            P(None, ("expert", "cuts")),
            P(None, ("expert", "cuts")),
            P(("expert", "cuts")),
            P(("expert", "cuts"), None),
            P(("expert", "cuts"), None),
            P(None, ("expert", "cuts")),
            P(("expert", "cuts")),
            P(None, ("expert", "cuts")),
            P(("expert", "cuts")),
            P(("expert", "cuts"), None),
            P(),
            P(),
            P(None, ("expert", "cuts")),
            P(None, ("expert", "cuts")),
            P(("expert", "cuts"), None),
        ),
        out_specs=(P(("group", "expert"), "cuts"), P("group", None, ("expert", "cuts"))),
        check_vma=False,
    )
```

```python
import functools

import jax
import jax.numpy as jnp
from jax import lax
from jax.experimental import pallas as pl
from jax.experimental.pallas import tpu as pltpu
from jax.sharding import PartitionSpec as P

EXPERTS = 2
DRAFT = 8
CAP = 16
F32 = jnp.float32
BF16 = jnp.bfloat16
VMEM_LIMIT = 28 << 20


def ring_place(index, owners):
    if owners == 8:
        low = index % 2
        return index // 2 * (1 - 2 * low) + 7 * low
    return index


def ring_index(place, owners):
    if owners == 8:
        low = place // 4
        return 2 * place * (1 - 2 * low) + 15 * low
    return place


def ring_perm(owners):
    pairs = []
    for index in range(owners):
        for core in range(2):
            to = ring_index((ring_place(index, owners) + 1 - 2 * core) % owners, owners)
            pairs.append((2 * index + core, 2 * to + core))
    return pairs


def ring_ahead(expert, core, owners):
    place = ring_place(expert, owners)
    return [
        ring_index(lax.rem(place + (1 - 2 * core) * d + owners, owners), owners)
        for d in range(owners // 2 + 1)
    ]


def over_cuts(value):
    return lax.ppermute(value, "cuts", [(0, 1), (1, 0)])


def over_expert(value, flip, owners):
    return lax.ppermute(value, "expert", [(i, i ^ flip) for i in range(owners)])


def rms_norm(values, gain):
    values = values.astype(F32)
    scale = lax.rsqrt(jnp.mean(values * values, axis=-1, keepdims=True) + 1e-05)
    return (values * scale * gain).astype(BF16)


def halves(first, second, core):
    return jnp.concatenate(
        [jnp.where(core == 0, first, second), jnp.where(core == 0, second, first)], axis=-1
    )


def gather_tokens(x_in, owners, core, ahead, behind, perm):
    half = owners // 2
    rows, width = x_in.shape

    def send(value):
        return lax.ppermute(value, ("expert", "cuts"), perm)

    other = over_cuts(x_in)
    part_a, part_b = [x_in], [other]
    for step in range(1, half + 1):
        part_a.append(send(part_a[-1]))
        if step < half:
            part_b.append(send(part_b[-1]))
    part_b, near = lax.optimization_barrier((part_b, part_a[:half]))
    part_a = [*near, part_a[half]]
    mine = [halves(part_a[d], part_b[d], core) for d in range(half)]
    stack = jnp.concatenate(mine[1:], axis=0)
    theirs = over_cuts(stack).reshape(half - 1, rows, 2 * width)
    far = halves(part_a[half], over_cuts(part_a[half]), core)
    out = jnp.zeros((owners * rows, 2 * width), x_in.dtype)

    def put(buffer, block, index):
        return lax.dynamic_update_slice(buffer, block, (index * rows, 0))

    out = put(out, mine[0], ahead[0])
    for d in range(1, half):
        out = put(out, mine[d], behind[d])
        out = put(out, theirs[d - 1], ahead[d])
    return put(out, far, ahead[half])


def sum_all(part, owners, expert, core, under):
    done = []

    def beside(value):
        if not under:
            return value
        value, extra = lax.optimization_barrier((value, under.pop(0)()))
        done.append(extra)
        return value

    def split(value, bit):
        size = value.shape[0] // 2
        return (
            lax.dynamic_slice_in_dim(value, bit * size, size, 0),
            lax.dynamic_slice_in_dim(value, (1 - bit) * size, size, 0),
        )

    def join(mine, theirs, bit):
        size = mine.shape[0]
        out = jnp.zeros((2 * size,) + mine.shape[1:], mine.dtype)
        out = lax.dynamic_update_slice_in_dim(out, mine, bit * size, 0)
        return lax.dynamic_update_slice_in_dim(out, theirs, (1 - bit) * size, 0)

    keep, give = split(part, core)
    keep = keep + over_cuts(give.astype(BF16)).astype(F32)
    low = expert % 2
    keep, give = split(keep, low)
    keep = keep + beside(over_expert(give.astype(BF16), 1, owners)).astype(F32)
    flip = 2
    while flip < owners:
        keep = keep + beside(over_expert(keep.astype(BF16), flip, owners)).astype(F32)
        flip *= 2
    keep = keep.astype(BF16)
    keep = join(keep, beside(over_expert(keep, 1, owners)), low)
    return (keep, over_cuts(keep)), done


def scan_kernel(
    place_ref,
    mine,
    theirs,
    dt_proj,
    dt_bias,
    u_ref,
    z_hbm,
    state_hbm,
    a_rate,
    d_skip,
    gated,
    new_state,
    notes,
    total,
    z_ref,
    state_ref,
    b_all,
    c_all,
    dt_all,
    sems,
):
    fetches = [
        pltpu.make_async_copy(state_hbm, state_ref, sems.at[0]),
        pltpu.make_async_copy(z_hbm, z_ref, sems.at[1]),
    ]
    for fetch in fetches:
        fetch.start()
    tokens, channels = u_ref.shape
    states = a_rate.shape[0]
    rank = dt_proj.shape[0]
    count = tokens // 2
    core = place_ref[place_ref.shape[0] - 1]
    total[pl.ds(pl.multiple_of(core * count, count), count), :] = mine[...]
    total[pl.ds(pl.multiple_of((1 - core) * count, count), count), :] = theirs[...]
    raw = jnp.dot(total[:, :rank], dt_proj[...], preferred_element_type=F32) + dt_bias[...]
    dt_all[...] = jnp.maximum(raw, 0.0) + jnp.log1p(jnp.exp(-jnp.abs(raw)))
    notes[...] = total[:, rank + 2 * states :].astype(F32)
    ones = jnp.ones((states, channels), BF16)
    diagonal = lax.broadcasted_iota(jnp.int32, (tokens, states, states), 1) == lax.broadcasted_iota(
        jnp.int32, (tokens, states, states), 2
    )
    maps = total[:, rank : rank + 2 * states].astype(F32)
    for start, dest in ((0, b_all), (states, c_all)):
        spread = jnp.broadcast_to(
            maps[:, None, start : start + states], (tokens, states, states)
        )
        spread = jnp.where(diagonal, spread, 0.0).reshape(tokens * states, states).astype(BF16)
        dest[...] = jnp.dot(spread, ones, preferred_element_type=F32)
    for fetch in fetches:
        fetch.wait()
    rate = -a_rate[...]
    skip = d_skip[...]

    def request(r, carry):
        at = pl.ds(pl.multiple_of(r * DRAFT, DRAFT), DRAFT)
        dt = dt_all[at, :]
        u = u_ref[at, :].astype(F32)
        du = dt * u
        state = state_ref[r]
        out = []
        for p in range(DRAFT):
            spot = pl.ds(pl.multiple_of((r * DRAFT + p) * states, states), states)
            state = jnp.exp(dt[p : p + 1] * rate) * state + du[p : p + 1] * b_all[spot, :]
            out.append(jnp.sum(c_all[spot, :] * state, axis=0, keepdims=True))
        new_state[r] = state
        z = z_ref[at, :]
        y = jnp.concatenate(out, axis=0) + skip * u
        gated[at, :] = y * (z * jax.nn.sigmoid(z))
        return carry

    lax.fori_loop(0, tokens // DRAFT, request, 0, unroll=8)


def scan(places, total, dt_proj, dt_bias, u, z, ssm_state, a_rate, d_skip):
    tokens, channels = u.shape
    states = a_rate.shape[0]
    columns = total[0].shape[1]
    extra = columns - dt_proj.shape[0] - 2 * states
    vmem = pl.BlockSpec(memory_space=pltpu.VMEM)
    return pl.pallas_call(
        scan_kernel,
        out_shape=(
            jax.ShapeDtypeStruct((tokens, channels), F32),
            jax.ShapeDtypeStruct(ssm_state.shape, F32),
            jax.ShapeDtypeStruct((tokens, extra), F32),
        ),
        in_specs=[pl.BlockSpec(memory_space=pltpu.SMEM)]
        + [vmem] * 5
        + [pl.BlockSpec(memory_space=pltpu.HBM)] * 2
        + [vmem] * 2,
        out_specs=[vmem] * 3,
        scratch_shapes=[
            pltpu.VMEM((tokens, columns), BF16),
            pltpu.VMEM((tokens, channels), F32),
            pltpu.VMEM(ssm_state.shape, F32),
            pltpu.VMEM((tokens * states, channels), F32),
            pltpu.VMEM((tokens * states, channels), F32),
            pltpu.VMEM((tokens, channels), F32),
            pltpu.SemaphoreType.DMA((2,)),
        ],
        compiler_params=pltpu.CompilerParams(vmem_limit_bytes=VMEM_LIMIT),
        name="scan",
    )(
        places,
        *total,
        dt_proj,
        dt_bias.reshape(1, -1),
        u,
        z,
        ssm_state,
        a_rate,
        d_skip.reshape(1, -1),
    )


def project_kernel(
    half, rows, width, place_ref, id_ref, g_ref, h_ref, wg_ref, wh_ref, near_ref, far_ref, own_ref, other_ref
):
    core = place_ref[half + 1]
    holders = 2 * half // EXPERTS
    ids = id_ref[...]
    column = lax.broadcasted_iota(jnp.int32, (1, (half + 1) * rows), 1)
    target = jnp.zeros_like(column)
    for d in range(half + 1):
        target = jnp.where(column // rows == d, place_ref[d], target)
    picked = (ids == slot_keys(target, column % rows, holders, rows)).astype(F32).astype(BF16)
    here = pl.multiple_of(core * width, 128)
    there = pl.multiple_of((1 - core) * width, 128)
    first = (((0,), (0,)), ((), ()))
    lhs_g = lax.dot_general(picked, g_ref[...], first, preferred_element_type=F32).astype(BF16)
    lhs_h = lax.dot_general(picked, h_ref[...], first, preferred_element_type=F32).astype(BF16)
    tile = 512
    for start in range(0, width, tile):
        at = pl.ds(here + start, tile)
        term = jnp.dot(lhs_g, wg_ref[:, at], preferred_element_type=F32) + jnp.dot(
            lhs_h, wh_ref[:, at], preferred_element_type=F32
        )
        own_ref[:, start : start + tile] = term[:rows]
        near_ref[:, start : start + tile] = term[rows : half * rows]
        far_ref[:, start : start + tile] = term[half * rows :].astype(BF16)
        at = pl.ds(there + start, tile)
        term = jnp.dot(
            lhs_g[rows : half * rows], wg_ref[:, at], preferred_element_type=F32
        ) + jnp.dot(lhs_h[rows : half * rows], wh_ref[:, at], preferred_element_type=F32)
        other_ref[:, start : start + tile] = term


def slots_kernel(routes_ref, out_ref):
    routes = routes_ref[...]
    count = routes.shape[0]
    named = [
        jnp.any(routes == label, axis=1, keepdims=True).astype(F32) for label in range(EXPERTS)
    ]
    idle = 1.0 - named[0] - named[1]
    lane = lax.broadcasted_iota(jnp.int32, (count, 128), 1)
    kinds = jnp.where(lane == 0, named[0], jnp.where(lane == 1, named[1], idle)).astype(BF16)
    earlier = (
        lax.broadcasted_iota(jnp.int32, (count, count), 0)
        > lax.broadcasted_iota(jnp.int32, (count, count), 1)
    )
    ranks = jnp.dot(
        earlier.astype(F32).astype(BF16), kinds, preferred_element_type=F32
    )
    first = jnp.sum(named[0], axis=0, keepdims=True)
    second = jnp.sum(named[1], axis=0, keepdims=True)
    spare = jnp.where(second < CAP, CAP + second, first)
    slot = (
        named[0] * ranks[:, 0:1]
        + named[1] * (CAP + ranks[:, 1:2])
        + idle * (spare + ranks[:, 2:3])
    )
    both = routes.astype(F32)
    out_ref[...] = jnp.concatenate([slot, both], axis=1)


def find_slots(routes):
    vmem = pl.BlockSpec(memory_space=pltpu.VMEM)
    return pl.pallas_call(
        slots_kernel,
        out_shape=jax.ShapeDtypeStruct((routes.shape[0], 1 + routes.shape[1]), F32),
        in_specs=[vmem],
        out_specs=vmem,
        compiler_params=pltpu.CompilerParams(vmem_limit_bytes=1 << 20),
        name="slots",
    )(routes)


def slot_keys(target, row, holders, rows):
    expert = target // holders
    block = jnp.where(row < CAP, target, target + holders * (1 - 2 * expert))
    return block * rows + expert * CAP + row % CAP


def project_blocks(ids, gated, gated_other, out_proj, out_other, rows, half, places):
    width = out_proj.shape[1] // 2
    vmem = pl.BlockSpec(memory_space=pltpu.VMEM)
    return pl.pallas_call(
        functools.partial(project_kernel, half, rows, width),
        out_shape=(
            jax.ShapeDtypeStruct(((half - 1) * rows, width), F32),
            jax.ShapeDtypeStruct((rows, width), BF16),
            jax.ShapeDtypeStruct((rows, width), F32),
            jax.ShapeDtypeStruct(((half - 1) * rows, width), F32),
        ),
        in_specs=[pl.BlockSpec(memory_space=pltpu.SMEM)] + [vmem] * 5,
        out_specs=[vmem] * 4,
        compiler_params=pltpu.CompilerParams(vmem_limit_bytes=14 << 20),
        name="project",
    )(places, ids, gated, gated_other, out_proj, out_other)


def scatter_sum(near, far, own, other, rows, owners, perm):
    half = owners // 2

    def send(value):
        return lax.ppermute(value.astype(BF16), ("expert", "cuts"), perm)

    acc_a = send(far)
    acc_b = None
    for d in range(half - 1, 0, -1):
        at = slice((d - 1) * rows, d * rows)
        acc_a = send(acc_a.astype(F32) + near[at])
        acc_b = send(other[at] if acc_b is None else acc_b.astype(F32) + other[at])
    return own + acc_a.astype(F32) + over_cuts(acc_b).astype(F32)


def experts_kernel(tiles, pieces, place_ref, *refs):
    own, refs = refs[:pieces], refs[pieces:]
    other, refs = refs[:pieces], refs[pieces:]
    gain_ref, wg_hbm, wu_hbm, wd_hbm, out_ref, x_ref, wg, wu, wd, sems = refs
    depth = wg.shape[0] // tiles
    inner = wd.shape[0] // tiles

    def fetch(kind, src, dst, size):
        parts = [pl.ds(i * size, size) for i in range(tiles)]
        return [
            pltpu.make_async_copy(src.at[at, :], dst.at[at, :], sems.at[kind, i])
            for i, at in enumerate(parts)
        ]

    gates = fetch(0, wg_hbm, wg, depth)
    ups = fetch(1, wu_hbm, wu, depth)
    downs = fetch(2, wd_hbm, wd, inner)
    for i in range(tiles):
        gates[i].start()
        ups[i].start()
    for copy in downs:
        copy.start()
    rows, width = own[0].shape
    core = place_ref[place_ref.shape[0] - 1]
    here = pl.ds(pl.multiple_of(core * width, 128), width)
    there = pl.ds(pl.multiple_of((1 - core) * width, 128), width)
    for i in range(pieces):
        x_ref[i * rows : (i + 1) * rows, here] = own[i][...]
        x_ref[i * rows : (i + 1) * rows, there] = other[i][...]
    values = x_ref[...].astype(F32)
    scale = lax.rsqrt(jnp.mean(values * values, axis=-1, keepdims=True) + 1e-05)
    x_ref[...] = (values * scale * gain_ref[...]).astype(BF16)
    gate = upval = None
    for i in range(tiles):
        at = slice(i * depth, (i + 1) * depth)
        gates[i].wait()
        term = jnp.dot(x_ref[:, at], wg[at, :], preferred_element_type=F32)
        gate = term if gate is None else gate + term
        ups[i].wait()
        term = jnp.dot(x_ref[:, at], wu[at, :], preferred_element_type=F32)
        upval = term if upval is None else upval + term
    act = (gate * jax.nn.sigmoid(gate) * upval).astype(BF16)
    for i in range(tiles):
        at = slice(i * inner, (i + 1) * inner)
        downs[i].wait()
        term = jnp.dot(act[:, at], wd[at, :], preferred_element_type=F32)
        if i == 0:
            out_ref[...] = term
        else:
            out_ref[...] += term


def run_experts(places, own, other, gain, w_gate, w_up, w_down):
    pieces = len(own)
    count, width = pieces * own[0].shape[0], 2 * own[0].shape[1]
    tiles = 4
    vmem = pl.BlockSpec(memory_space=pltpu.VMEM)
    hbm = pl.BlockSpec(memory_space=pltpu.HBM)
    return pl.pallas_call(
        functools.partial(experts_kernel, tiles, pieces),
        out_shape=jax.ShapeDtypeStruct((count, width), F32),
        in_specs=[pl.BlockSpec(memory_space=pltpu.SMEM)] + [vmem] * (2 * pieces + 1) + [hbm] * 3,
        out_specs=vmem,
        scratch_shapes=[
            pltpu.VMEM((count, width), BF16),
            pltpu.VMEM(w_gate.shape, BF16),
            pltpu.VMEM(w_up.shape, BF16),
            pltpu.VMEM(w_down.shape, BF16),
            pltpu.SemaphoreType.DMA((3, tiles)),
        ],
        compiler_params=pltpu.CompilerParams(vmem_limit_bytes=28 << 20),
        name="experts",
    )(
        places,
        *own,
        *other,
        gain.reshape(1, width),
        *(pltpu.with_memory_space_constraint(w, pltpu.HBM) for w in (w_gate, w_up, w_down)),
    )


def on_device(
    x_in,
    routes,
    conv_state,
    ssm_state,
    mamba_gain,
    in_x,
    in_z,
    conv_w,
    conv_b,
    xproj_dt,
    xproj_bc,
    dt_proj,
    dt_bias,
    a_rate,
    d_skip,
    out_proj,
    moe_gain,
    router,
    w_gate,
    w_up,
    w_down,
):
    tok_count, half_width = x_in.shape
    requests = conv_state.shape[0]
    channels = in_x.shape[1]
    owners = lax.axis_size("expert")
    expert = lax.axis_index("expert")
    core = lax.axis_index("cuts")
    half = owners // 2
    perm = ring_perm(owners)
    ahead = ring_ahead(expert, core, owners)
    behind = ring_ahead(expert, 1 - core, owners)
    places = jnp.stack(ahead + [core]).astype(jnp.int32)
    out_other = over_cuts(out_proj)
    full_x = gather_tokens(x_in, owners, core, ahead, behind, perm)
    normed = rms_norm(full_x, mamba_gain)
    u_pre = jnp.dot(normed, in_x, preferred_element_type=F32)
    seq = jnp.concatenate([conv_state, u_pre.reshape(requests, DRAFT, channels)], axis=1)
    conv = jnp.zeros((requests, DRAFT, channels), F32) + conv_b
    for tap in range(conv_w.shape[0]):
        conv = conv + conv_w[tap] * seq[:, tap : tap + DRAFT]
    u_act = jax.nn.silu(conv).astype(BF16)
    flat_u = u_act.reshape(requests * DRAFT, channels)
    rank = xproj_dt.shape[1]
    notes = find_slots(routes)
    slot = notes[:, 0]
    notes = jnp.where(core == 0, notes, 0.0)
    tokens = flat_u.shape[0]
    notes = lax.dynamic_update_slice(
        jnp.zeros((tokens, notes.shape[1]), F32), notes, (expert * tok_count, 0)
    )
    part = jnp.concatenate(
        [
            jnp.dot(flat_u, xproj_dt, preferred_element_type=F32),
            jnp.dot(flat_u, xproj_bc, preferred_element_type=F32),
            notes,
        ],
        axis=1,
    )
    holders = owners // EXPERTS
    own = expert // holders
    partner = expert + holders * (1 - 2 * own)
    x_partner = lax.dynamic_slice(
        full_x, (partner * tok_count, core * half_width), (tok_count, half_width)
    )
    part, x_partner = lax.optimization_barrier((part, x_partner))
    total, (z_gate,) = sum_all(
        part,
        owners,
        expert,
        core,
        [lambda: jnp.dot(normed, in_z, preferred_element_type=F32)],
    )
    gated, new_state, notes = scan(
        places, total, dt_proj, dt_bias, flat_u, z_gate, ssm_state, a_rate, d_skip
    )
    gated = gated.astype(BF16)
    ids = (jnp.arange(tokens) // tok_count * tok_count).astype(jnp.int32)[:, None] + notes[
        :, :1
    ].astype(jnp.int32)
    near, far, own_term, other = project_blocks(
        ids,
        gated,
        over_cuts(gated),
        out_proj,
        out_other,
        tok_count,
        half,
        places,
    )
    row = jnp.arange(tok_count, dtype=jnp.int32)
    rows_here = (slot_keys(expert, row, holders, tok_count)[:, None] == ids[:, 0][None, :]).astype(
        BF16
    )
    x_rows = jnp.dot(
        lax.dynamic_slice_in_dim(rows_here, expert * tok_count, tok_count, 1),
        x_in,
        preferred_element_type=F32,
    ) + jnp.dot(
        lax.dynamic_slice_in_dim(rows_here, partner * tok_count, tok_count, 1),
        x_partner,
        preferred_element_type=F32,
    )
    route_rows = jnp.dot(rows_here, notes[:, 1:].astype(BF16), preferred_element_type=F32).astype(jnp.int32)
    mixed_half = scatter_sum(near, far, own_term, other, tok_count, owners, perm)
    stream_half = (x_rows + mixed_half).astype(BF16)

    def exchange(value, flip):
        return over_expert(value, flip, owners)

    pieces = [stream_half] + [exchange(stream_half, flip) for flip in range(1, holders)]
    others = [over_cuts(piece) for piece in pieces]
    partial_out = run_experts(places, pieces, others, moe_gain, w_gate, w_up, w_down)
    count = partial_out.shape[0]
    mine = lax.dynamic_slice(partial_out, (0, core * half_width), (count, half_width))
    theirs = lax.dynamic_slice(partial_out, (0, (1 - core) * half_width), (count, half_width))
    summed = mine + over_cuts(theirs.astype(BF16)).astype(F32)
    summed = summed.reshape(holders, 2 * CAP, half_width)
    result = summed[0]
    for flip in range(1, holders):
        result = result + exchange(summed[flip].astype(BF16), flip).astype(F32)
    expert_out = result.astype(BF16).astype(F32)

    logits = jnp.dot(
        rms_norm(halves(stream_half, others[0], core), moe_gain), router, preferred_element_type=F32
    )
    all_labels = jnp.arange(router.shape[1], dtype=jnp.int32)
    which = (route_rows[:, :, None] == all_labels).astype(F32)
    chosen = jnp.sum(logits[:, None, :] * which, axis=-1)
    weight0 = jax.nn.sigmoid(chosen[:, 0] - chosen[:, 1])
    weights = jnp.stack([weight0, 1.0 - weight0], axis=1)
    weight = jnp.sum(jnp.where(route_rows < EXPERTS, weights, 0.0), axis=1)
    done = (stream_half.astype(F32) + weight[:, None] * expert_out).astype(BF16)
    back = exchange(done[CAP:], holders)
    table = jnp.concatenate([done[:CAP], back], axis=0)
    wanted = slot.astype(jnp.int32)
    wanted = jnp.where(own == 0, wanted, (wanted + CAP) % (EXPERTS * CAP))
    pick = (wanted[:, None] == row[None, :]).astype(BF16)
    out = jnp.dot(pick, table, preferred_element_type=F32).astype(BF16)
    return (out, new_state)


def solution(mesh):
    return jax.shard_map(
        on_device,
        mesh=mesh,
        in_specs=(
            P(("group", "expert"), "cuts"),
            P(("group", "expert"), None),
            P("group", None, ("expert", "cuts")),
            P("group", None, ("expert", "cuts")),
            P(),
            P(None, ("expert", "cuts")),
            P(None, ("expert", "cuts")),
            P(None, ("expert", "cuts")),
            P(("expert", "cuts")),
            P(("expert", "cuts"), None),
            P(("expert", "cuts"), None),
            P(None, ("expert", "cuts")),
            P(("expert", "cuts")),
            P(None, ("expert", "cuts")),
            P(("expert", "cuts")),
            P(("expert", "cuts"), None),
            P(),
            P(),
            P(None, ("expert", "cuts")),
            P(None, ("expert", "cuts")),
            P(("expert", "cuts"), None),
        ),
        out_specs=(P(("group", "expert"), "cuts"), P("group", None, ("expert", "cuts"))),
        check_vma=False,
    )
```
